32 devices in a mesh: expert: 8 (over y, x, core), dp: 4 (over z).
Axes of the slice: x: 2, y: 2, z: 4, core: 2. Of those that a mesh axis runs over, the one named last changes fastest.
Arguments:
- tokens: bfloat16 [512, 2048], P(('expert', 'dp')), may hold values from -6 to 6
- out_grad: bfloat16 [512, 2048], P(('expert', 'dp')), may hold values from -6 to 6
- routes: int32 [512, 8], P(('expert', 'dp')), may hold values from 0 to 15, all different within a row; in each aligned block of 16 rows (0 to 15, 16 to 31, ...) at most 16 rows name the same one
- route_gates: float32 [512, 8], P(('expert', 'dp')), may hold values from 0.05 to 0.5
- w_gate: bfloat16 [16, 2048, 384], P('expert'), may hold values from -0.125 to 0.125
- w_up: bfloat16 [16, 2048, 384], P('expert'), may hold values from -0.125 to 0.125
- w_down: bfloat16 [16, 384, 2048], P('expert'), may hold values from -0.3125 to 0.3125
Outputs:
- token_grad: bfloat16 [512, 2048], P(('expert', 'dp'))
- down_grad: float32 [384, 16, 2048], P('dp', 'expert')
The draws below stay inside these ranges and needn't reach their ends.
Inputs may be any that keep to these rules, and one draw needn't show every extreme that they name: `routes`: each row names 8 different experts. Among the 16 tokens of one device no expert is named more than 16 times, a bound that some block reaches.
All inputs are finite; a program needn't handle non-finite values.
Results may differ from the reference program's by a relative error of at most 0.014.
Values may be sent and summed in bfloat16 or wider, within the bound.
A program may use at most 64 MiB of HBM per device.

```python
import math
import jax
import jax.numpy as jnp
import numpy as np
from jax import lax

D = 2048
TOP = 8
FF = 384
TOK_DEV = 16
EXPERTS = 16
CAP = 16
TOKENS = 512
N_EXPERT = 8
N_DP = 4


def block_levels(rng, dims, split, least, high):
    def one(dim, parts):
        steps = jax.random.uniform(jax.random.fold_in(jax.random.fold_in(rng, 6), dim), (parts,), jnp.float32, least / len(split), high / len(split))
        return jnp.repeat(jnp.exp(steps), dims[dim] // parts).reshape((-1,) + (1,) * (len(dims) - dim - 1))

    level = one(*split[0])
    for cut in split[1:]:
        level = level * one(*cut)
    return level


def routed_block(own_key, own, number, rows, amount, top, most, slope):
    sequence = jax.random.permutation(own_key, amount)
    packed, common = load_shares(amount, rows * top, most, slope, True), load_shares(amount, rows * top, most, slope, False)
    places = jnp.arange(amount)

    def named(tallies, offset_by):
        used = int((tallies > 0).sum())
        fixed = max(1, used // 4)
        passed = fixed + (places - fixed + offset_by * (used - fixed)) % max(1, amount - fixed)
        return jnp.zeros((amount,), jnp.int32).at[sequence[jnp.where(places < fixed, places, passed)]].set(jnp.asarray(tallies, jnp.int32))

    tallies = jnp.where(number % 4 == 0, named(packed, number // 4), named(common, number - number // 4 - 1))
    mixed = jax.random.permutation(jax.random.fold_in(own, 3), amount)
    source_of, taker = mixed[0:amount // 2 * 2:2], mixed[1:amount // 2 * 2:2]
    room = jnp.minimum(tallies[source_of] - 1, most - tallies[taker]) // 2
    room = jnp.where((source_of == sequence[0]) | (taker == sequence[0]) | (tallies[taker] == 0), 0, jnp.maximum(room, 0))
    passed = jax.random.randint(jax.random.fold_in(own, 4), (amount // 2,), 0, 1 << 20) % (room + 1)
    tallies = tallies.at[source_of].add(-passed).at[taker].add(passed)
    members = jnp.searchsorted(jnp.cumsum(tallies), jnp.arange(rows * top), side="right").astype(jnp.int32)
    grid = members.reshape(top, rows).T
    grid = grid[jax.random.permutation(jax.random.fold_in(own, 1), rows)]
    offset_by = jax.random.randint(jax.random.fold_in(own, 2), (rows, 1), 0, top)
    return jnp.take_along_axis(grid, (jnp.arange(top)[None, :] + offset_by) % top, axis=1)


def load_shares(count, total, most, slope, full):
    portions = [(1 << 20) // math.isqrt(rank ** slope) + 1 for rank in range(1, count + 1)]
    largest = most if full else min(most, max(-(-total // count), total * portions[0] // sum(portions)))
    least = 1 if total - largest >= count - 1 else 0
    counts, surplus = [largest] + [least] * (count - 1), total - largest - least * (count - 1)
    while surplus > 0:
        free = [i for i in range(1, count) if counts[i] < largest] or [i for i in range(1, count) if counts[i] < most]
        pool, remaining = sum([portions[i] for i in free]), surplus
        for i in free:
            extra = min(most - counts[i], max(1, remaining * portions[i] // pool), surplus)
            counts[i] = counts[i] + extra
            surplus = surplus - extra
    return np.array(counts)


def gaussian(rng, dims, scale, most, pieces=(), kind=jnp.bfloat16):
    values = scale * jax.random.normal(rng, dims, jnp.float32)
    if pieces:
        values = values * block_levels(rng, dims, pieces, -0.22, 0.18)
    return jnp.clip(values, -most, most).astype(kind)


def setup_inputs(seed: int = 0) -> dict:
    arg_keys = jax.random.split(jax.random.key(seed), 8)
    tokens = gaussian(arg_keys[0], (TOKENS, D), 1.0, 6.0, ((0, 32),))
    out_grad = gaussian(arg_keys[1], (TOKENS, D), 1.0, 6.0, ((0, 32),))
    routes_keys = jax.random.split(jax.random.fold_in(arg_keys[2], 1), TOKENS // TOK_DEV)
    routes_turns = jax.random.permutation(jax.random.fold_in(arg_keys[2], 3), TOKENS // TOK_DEV)
    routes = jax.vmap(lambda own, number: routed_block(jax.random.fold_in(arg_keys[2], 2), own, number, TOK_DEV, EXPERTS, TOP, CAP, 2))(routes_keys, routes_turns).reshape((TOKENS, TOP))
    route_gates = jnp.clip(jnp.exp(math.log(0.5) - 2.3025851 * jax.random.uniform(arg_keys[3], (TOKENS, TOP), jnp.float32) ** block_levels(arg_keys[3], (TOKENS, TOP), ((0, 32),), -0.2, 0.2)), 0.05, 0.5)
    w_gate = gaussian(arg_keys[4], (EXPERTS, D, FF), D ** -0.5, 0.125, ((0, 8),))
    w_up = gaussian(arg_keys[5], (EXPERTS, D, FF), D ** -0.5, 0.125, ((0, 8),))
    w_down = gaussian(arg_keys[6], (EXPERTS, FF, D), FF ** -0.5, 0.3125, ((0, 8),))
    return {"tokens": tokens, "out_grad": out_grad, "routes": routes, "route_gates": route_gates, "w_gate": w_gate, "w_up": w_up, "w_down": w_down}


def reference(tokens, out_grad, routes, route_gates, w_gate, w_up, w_down):
    span = TOK_DEV * TOP
    limit = N_EXPERT * span
    most_rows = N_EXPERT * CAP
    group_routes = routes.reshape(N_EXPERT, N_DP, span).transpose(1, 0, 2).reshape(N_DP, limit)
    dp_iota = jnp.arange(N_DP, dtype=jnp.int32)

    def expert_pass(carry, inputs):
        expert_id, gate_mat, up_mat, down_mat = inputs
        hits = group_routes == expert_id
        positions = jax.vmap(lambda m: jnp.nonzero(m, size=most_rows, fill_value=limit)[0])(hits).astype(jnp.int32)
        valid = positions < limit
        safe = jnp.where(valid, positions, 0).astype(jnp.int32)
        owner = safe // span
        local = (safe // TOP) % TOK_DEV
        choice_k = safe % TOP
        token_index = ((owner * N_DP + dp_iota[:, None]) * TOK_DEV + local).astype(jnp.int32)
        x_rows = jnp.where(valid[..., None], tokens[token_index], jnp.zeros((), tokens.dtype))
        gain = jnp.where(valid, route_gates[token_index, choice_k], 0.0)
        dy_rows = (gain[..., None] * out_grad[token_index].astype(jnp.float32)).astype(jnp.bfloat16)
        x32 = x_rows.astype(jnp.float32)
        dy32 = dy_rows.astype(jnp.float32)
        gate_pre = jnp.einsum('pmd,df->pmf', x32, gate_mat.astype(jnp.float32))
        up_pre = jnp.einsum('pmd,df->pmf', x32, up_mat.astype(jnp.float32))
        sigmoid_gate = jax.nn.sigmoid(gate_pre)
        silu_gate = gate_pre * sigmoid_gate
        hidden = (silu_gate * up_pre).astype(jnp.bfloat16)
        hidden_grad = jnp.einsum('pmd,fd->pmf', dy32, down_mat.astype(jnp.float32))
        gate_grad = (hidden_grad * up_pre * (sigmoid_gate + gate_pre * sigmoid_gate * (1.0 - sigmoid_gate))).astype(jnp.bfloat16)
        up_grad = (hidden_grad * silu_gate).astype(jnp.bfloat16)
        row_grad = (jnp.einsum('pmf,df->pmd', gate_grad.astype(jnp.float32), gate_mat.astype(jnp.float32))
                    + jnp.einsum('pmf,df->pmd', up_grad.astype(jnp.float32), up_mat.astype(jnp.float32))).astype(jnp.bfloat16)
        part = jnp.einsum('pmf,pmd->pfd', hidden.astype(jnp.float32), dy32).astype(jnp.bfloat16)
        part = lax.optimization_barrier(part)
        down_part = jnp.sum(part.astype(jnp.float32), axis=0)
        added = jnp.where(valid[..., None], row_grad.astype(jnp.float32), 0.0)
        carry = carry.at[token_index.reshape(-1)].add(added.reshape(-1, D))
        return carry, down_part

    start_grad = jnp.zeros((TOKENS, D), jnp.float32)
    expert_ids = jnp.arange(EXPERTS, dtype=jnp.int32)
    token_grad, downs = lax.scan(expert_pass, start_grad, (expert_ids, w_gate, w_up, w_down))
    return token_grad.astype(jnp.bfloat16), jnp.transpose(downs, (1, 0, 2))
```

```python
import functools

import jax
import jax.numpy as jnp
from jax import lax
from jax.experimental import pallas as pl
from jax.experimental.pallas import tpu as pltpu
from jax.sharding import PartitionSpec as P

VMEM_BUDGET = 56 << 20
VMEM_PASSED = 4 << 20
STEPS = 2
PARTS = 4
HALVES = 2
ALONG = ((3, 0), (3, 1))
MESH = pl.DeviceIdType.MESH
NT = (((1,), (1,)), ((), ()))


def gate_up(arrived, w_gate, w_up):
    gate_pre = jnp.einsum("erd,edf->erf", arrived, w_gate, preferred_element_type=jnp.float32)
    up_pre = jnp.einsum("erd,edf->erf", arrived, w_up, preferred_element_type=jnp.float32)
    return (gate_pre, up_pre)


def collective_shards(tokens, out_grad, routes, route_gates, w_gate, w_up, w_down):
    tok_count, model_width = tokens.shape
    top_count = routes.shape[1]
    local_experts = w_gate.shape[0]
    groups = lax.axis_size("expert")
    experts = local_experts * groups
    slot_count = 2 * tok_count * top_count // experts
    flat_routes = routes.reshape(-1)
    onehot = (flat_routes[:, None] == jnp.arange(experts, dtype=jnp.int32)[None, :]).astype(
        jnp.int32
    )
    slot_rank = jnp.sum(onehot * (jnp.cumsum(onehot, axis=0) - onehot), axis=1)
    slot_index = flat_routes * slot_count + slot_rank
    placement = slot_index[None, :] == jnp.arange(experts * slot_count, dtype=jnp.int32)[:, None]
    route_place = placement.astype(jnp.bfloat16)
    token_place = jnp.sum(
        placement.reshape(experts * slot_count, tok_count, top_count).astype(jnp.float32), axis=2
    ).astype(jnp.bfloat16)
    send_inputs = (
        jnp.dot(token_place, tokens, preferred_element_type=jnp.float32)
        .astype(jnp.bfloat16)
        .reshape(experts, slot_count, model_width)
    )
    scaled = (
        (route_gates[:, :, None] * out_grad[:, None, :].astype(jnp.float32))
        .astype(jnp.bfloat16)
        .reshape(tok_count * top_count, model_width)
    )
    send_grads = (
        jnp.dot(route_place, scaled, preferred_element_type=jnp.float32)
        .astype(jnp.bfloat16)
        .reshape(experts, slot_count, model_width)
    )
    arrived, arrived_grad = (
        lax.all_to_all(send_inputs, "expert", split_axis=0, concat_axis=1, tiled=True),
        lax.all_to_all(send_grads, "expert", split_axis=0, concat_axis=1, tiled=True),
    )
    gate_pre, up_pre = gate_up(arrived, w_gate, w_up)
    sigmoid_gate = jax.nn.sigmoid(gate_pre)
    silu_gate = gate_pre * sigmoid_gate
    hidden = (silu_gate * up_pre).astype(jnp.bfloat16)
    hidden_grad = jnp.einsum(
        "erd,efd->erf", arrived_grad, w_down, preferred_element_type=jnp.float32
    )
    gate_grad = (
        hidden_grad * up_pre * (sigmoid_gate + gate_pre * sigmoid_gate * (1.0 - sigmoid_gate))
    ).astype(jnp.bfloat16)
    up_grad = (hidden_grad * silu_gate).astype(jnp.bfloat16)
    row_grads = (
        jnp.einsum("erf,edf->erd", gate_grad, w_gate, preferred_element_type=jnp.float32)
        + jnp.einsum("erf,edf->erd", up_grad, w_up, preferred_element_type=jnp.float32)
    ).astype(jnp.bfloat16)
    returned = lax.all_to_all(row_grads, "expert", split_axis=1, concat_axis=0, tiled=True)
    token_grad = lax.dot_general(
        token_place,
        returned.reshape(experts * slot_count, model_width),
        (((0,), (0,)), ((), ())),
        preferred_element_type=jnp.float32,
    ).astype(jnp.bfloat16)
    hidden_units = hidden.shape[2]
    share_rows = hidden_units // lax.axis_size("dp")
    partial_grad = jnp.einsum(
        "erf,erd->fed", hidden, arrived_grad, preferred_element_type=jnp.float32
    ).astype(jnp.bfloat16)
    total_grad = lax.psum(partial_grad, "dp").astype(jnp.float32)
    first_row = lax.axis_index("dp") * share_rows
    down_grad = lax.dynamic_slice_in_dim(total_grad, first_row, share_rows, 0)
    return (token_grad, down_grad)


def flip(index, bits):
    out, step = index, 1
    while step <= bits:
        if bits & step:
            out = out + step * (1 - 2 * ((index // step) % 2))
        step *= 2
    return out


def copy_keys(chips, planes, local_experts):
    keys = [("z", k) for k in range(1, planes)] + [("m", i) for i in range(2)]
    for name in ("r", "g"):
        keys += [(name, d) for d in range(1, chips)] + [(name + "c", d) for d in range(chips)]
    keys += [("x", d, h) for d in range(1, chips) for h in range(HALVES)]
    keys += [("xc", d, h) for d in range(chips) for h in range(HALVES)]
    keys += [("d", k, d, h) for k in range(planes) for d in range(1, chips) for h in range(HALVES)]
    keys += [("dc", 0, d, h) for d in range(chips) for h in range(HALVES)]
    keys += [("dc", k, d) for k in range(1, planes) for d in range(chips)]
    keys += [("h", k, e) for k in range(1, planes) for e in range(local_experts)]
    keys += [("p", j) for j in range(PARTS)]
    keys += [("t", j, d) for j in range(PARTS) for d in range(1, chips)]
    return {key: i for i, key in enumerate(keys)}


def fused_kernel(
    chips, planes, tok, dy, rt, gt, wg, wu, wd, every, hid_in, own_sum, ret_in,
    xb, rb, gb, wide, wdv, pre, grads, hid_f, hid_out, both,
    keep, pair_out, pair_in, ret_out, lsem, ssem, rsem, known,
):
    local_experts, model_width, hidden_units = wg.shape
    rows = tok.shape[0]
    count = 2 * chips * rows
    share = hidden_units // planes
    width = model_width // PARTS
    half = model_width // HALVES
    me, plane = lax.axis_index("expert"), lax.axis_index("dp")
    chip, core = me // 2, me % 2
    inner = (plane % 2) != (plane // 2)
    partner = {"expert": chip * 2 + 1 - core, "dp": plane}
    across = [{"expert": flip(chip, d) * 2 + core, "dp": plane} for d in range(chips)]
    above = [{"expert": me, "dp": flip(plane, k)} for k in range(planes)]
    keys = copy_keys(chips, planes, local_experts)

    local = []

    def load(src, dst):
        c = pltpu.make_async_copy(src, dst, lsem.at[len(local)])
        c.start()
        local.append(c)
        return c

    own = [load(tok, xb.at[0]), load(rt, rb.at[0]), load(gt, gb.at[0]), load(dy, every.at[0, 0])]
    down_loads = [
        load(wd.at[e], wdv.at[pl.ds(e * hidden_units, hidden_units)]) for e in range(local_experts)
    ]
    gate_up_loads = []
    for e in range(local_experts):
        for i, w in enumerate((wg, wu)):
            gate_up_loads.append(
                load(w.at[e], wide.at[:, pl.ds((2 * e + i) * hidden_units, hidden_units)])
            )

    def remote(key, src, dst, target, arrives=None):
        return pltpu.make_async_remote_copy(
            src_ref=src, dst_ref=dst, send_sem=ssem.at[keys[key]],
            recv_sem=rsem.at[keys[arrives or key]], device_id=target, device_id_type=MESH,
        )

    def cols(h):
        return pl.ds(h * half, half)

    copies, inner_copies = {}, {}
    for name, src, buf in (("r", rt, rb), ("g", gt, gb)):
        for d in range(chips):
            if d:
                copies[name, d] = remote((name, d), src, buf.at[2 * d], across[d])
            copies[name + "c", d] = remote(
                (name + "c", d), buf.at[2 * d] if d else src, buf.at[2 * d + 1], partner
            )

    def spread(name, first, buf, lead):
        for h in range(HALVES):
            for d in (1, 2):
                copies[(name,) + lead + (d, h)] = remote(
                    (name,) + lead + (d, h), first.at[:, cols(h)], buf.at[2 * d, :, cols(h)], across[d]
                )
            via, to = (1, 2) if h == 0 else (2, 1)
            copies[(name,) + lead + (3, h)] = remote(
                (name,) + lead + (3, h), buf.at[2 * via, :, cols(h)], buf.at[6, :, cols(h)], across[to]
            )

    spread("x", tok, xb, ())
    for d in range(chips):
        for h in range(HALVES):
            for key, first, buf in ((("xc",), tok, xb), (("dc", 0), dy, every.at[0])):
                copies[key + (d, h)] = remote(
                    key + (d, h),
                    buf.at[2 * d, :, cols(h)] if d else first.at[:, cols(h)],
                    buf.at[2 * d + 1, :, cols(h)],
                    partner,
                )
    for k in range(planes):
        spread("d", every.at[k, 0] if k else dy, every.at[k], (k,))
        if k:
            for d in range(chips):
                copies["dc", k, d] = remote(
                    ("dc", k, d), every.at[k, 2 * d], every.at[k, 2 * d + 1], partner
                )
            copies["z", k] = remote(("z", k), dy, every.at[k, 0], above[k])
    for d, h in ALONG:
        copies["d", 1, d, h] = remote(
            ("d", 1, d, h), every.at[0, 2 * d, :, cols(h)], every.at[1, 2 * d, :, cols(h)], above[1]
        )
    for k in range(1, planes):
        first = pl.multiple_of(flip(plane, k) * share, 16)
        for e in range(local_experts):
            copies["h", k, e] = remote(
                ("h", k, e), hid_out.at[e, pl.ds(first, share)], hid_in.at[k, e], above[k]
            )
    for j in range(PARTS):
        copies["p", j] = remote(("p", j), pair_out.at[j], pair_in.at[j], partner)
        for d in range(1, chips):
            copies["t", j, d] = remote(
                ("t", j, d), ret_out.at[j, d], ret_in.at[d - 1, :, pl.ds(j * width, width)], across[d]
            )

    def start(*key):
        copies[key].start()

    def arrive(*key):
        copies[key].wait_recv()

    def relay(name, lead=()):
        for d, h in ((1, 0), (2, 1)):
            arrive(name, *lead, d, h)
            if name == "x" or lead[0] != 1 or (3, h) not in ALONG:
                start(name, *lead, 3, h)
            if name == "x" or lead[0] == 0:
                start(name + "c", *lead, d, h)

    def rest(name, lead=()):
        for d, h in ((1, 1), (2, 0)):
            arrive(name, *lead, d, h)
            if name == "x" or lead[0] == 0:
                start(name + "c", *lead, d, h)
            else:
                start("dc", *lead, d)

    def send_plane(k):
        for h in range(HALVES):
            for d in (1, 2):
                piece = (d, h if d == 1 else 1 - h)
                if k != 1 or piece not in ALONG:
                    start("d", k, *piece)

    barrier = pltpu.get_barrier_semaphore()
    for target in [partner] + across[1:3] + [above[1]]:
        pl.semaphore_signal(barrier, inc=1, device_id=target, device_id_type=MESH)

    @pl.when(inner)
    def _():
        pl.semaphore_signal(barrier, inc=1, device_id=above[3], device_id_type=MESH)

    pl.semaphore_wait(barrier, 4 + inner.astype(jnp.int32))

    @pl.when(inner)
    def _():
        pl.semaphore_signal(known, inc=1, device_id=above[3], device_id_type=MESH)
        copies["z", 3].start()

    send_plane(0)
    start("z", 1)
    for h in range(HALVES):
        start("dc", 0, 0, h)
    for name in ("r", "g"):
        for d in (1, 2):
            start(name, d)
        start(name + "c", 0)
    for h in range(HALVES):
        start("x", 1, h)
        start("x", 2, 1 - h)
        start("xc", 0, h)

    @pl.when(inner)
    def _():
        pl.semaphore_wait(known, 1)
        pl.semaphore_signal(known, inc=1, device_id=above[1], device_id_type=MESH)
        copies["z", 2].start()

    relay("d", (0,))
    rest("d", (0,))
    for name in ("r", "g"):
        start(name, 3)

    @pl.when(jnp.logical_not(inner))
    def _():
        pl.semaphore_wait(known, 1)
        copies["z", 3].start()
        copies["z", 2].start()

    relay("x")
    rest("x")
    for name in ("r", "g"):
        for d in (1, 2):
            arrive(name, d)
            start(name + "c", d)
    arrive("z", 1)
    send_plane(1)
    start("dc", 1, 0)
    for h in range(HALVES):
        arrive("d", 0, 3, h)
        start("dc", 0, 3, h)
    for d, h in ALONG:
        start("d", 1, d, h)
    for h in range(HALVES):
        arrive("x", 3, h)
        start("xc", 3, h)
    for name in ("r", "g"):
        arrive(name, 3)
        start(name + "c", 3)

    for c in own:
        c.wait()
    for c in down_loads:
        c.wait()
    for h in range(HALVES):
        for d in range(chips):
            arrive("dc", 0, d, h)
        begin = h * half
        term = lax.dot_general(
            wdv[:, begin : begin + half],
            every[0, :, :, begin : begin + half].reshape(count, half),
            NT,
            preferred_element_type=jnp.float32,
        ).T
        grads[...] = grads[...] + term if h else term
    arrive("z", 2)
    send_plane(2)
    start("dc", 2, 0)
    for c in gate_up_loads:
        c.wait()
    for h in range(HALVES):
        for d in range(chips):
            arrive("xc", d, h)
        begin = h * half
        term = jnp.dot(
            xb[:, :, begin : begin + half].reshape(count, half),
            wide[begin : begin + half, :],
            preferred_element_type=jnp.float32,
        )
        pre[...] = pre[...] + term if h else term
        if h == 0:
            relay("d", (1,))
    arrive("z", 3)
    send_plane(3)
    start("dc", 3, 0)
    for name in ("r", "g"):
        for d in range(chips):
            arrive(name + "c", d)

    named, given = rb[...], gb[...]
    diagonal = lax.broadcasted_iota(jnp.int32, (1, rows, rows), 1) == lax.broadcasted_iota(
        jnp.int32, (1, rows, rows), 2
    )
    for e in range(local_experts):
        gain = jnp.sum(
            jnp.where(named == me * local_experts + e, given, 0.0), axis=1, keepdims=True
        )
        gain = jnp.sum(jnp.where(diagonal, gain, 0.0), axis=2, keepdims=True).reshape(count, 1)
        a, b, c = ((2 * e + i) * hidden_units for i in range(3))
        hidden_grad = gain * grads[:, e * hidden_units : (e + 1) * hidden_units]
        gate_pre, up_pre = pre[:, a:b], pre[:, b:c]
        s = jax.nn.sigmoid(gate_pre)
        silu = gate_pre * s
        hid_f[e] = silu * up_pre * gain
        both[:, a:b] = (hidden_grad * up_pre * (s + gate_pre * s * (1.0 - s))).astype(jnp.bfloat16)
        both[:, b:c] = (hidden_grad * silu).astype(jnp.bfloat16)

    hid_loads = []
    for j in range(PARTS + 1):
        if j < PARTS:
            total = lax.dot_general(
                wide[j * width : (j + 1) * width, :], both[...], NT, preferred_element_type=jnp.float32
            ).T.reshape(chips, 2, rows, width)
            pair_out[j] = total[:, 1].astype(jnp.bfloat16)
            start("p", j)
            keep[j] = total[:, 0]
        if j == 0:
            rest("d", (1,))
        if j == 1:
            for e in range(local_experts):
                hid_out[e] = hid_f[e].T.astype(jnp.bfloat16)
            for k in range(1, planes):
                for e in range(local_experts):
                    start("h", k, e)
            first = pl.multiple_of(plane * share, 16)
            for e in range(local_experts):
                hid_loads.append(load(hid_out.at[e, pl.ds(first, share)], hid_in.at[0, e]))
            relay("d", (2,))
        if j == 2:
            rest("d", (2,))
        if j == 3:
            relay("d", (3,))
        if j:
            i = j - 1
            arrive("p", i)
            total = keep[i] + pair_in[i].astype(jnp.float32)
            for d in range(chips - 1, 0, -1):
                ret_out[i, d] = total[d].astype(jnp.bfloat16)
            for d in range(chips - 1, 0, -1):
                start("t", i, d)
            own_sum[:, i * width : (i + 1) * width] = total[0]

    rest("d", (3,))
    for k in range(1, planes):
        for h in range(HALVES):
            arrive("d", k, 3, h)
        start("dc", k, 3)
    for k in range(1, planes):
        for e in range(local_experts):
            arrive("h", k, e)
        for d in range(chips):
            arrive("dc", k, d)
    for j in range(PARTS):
        for d in range(1, chips):
            arrive("t", j, d)
    for c in hid_loads:
        c.wait()
    for c in copies.values():
        c.wait_send()


def finish_kernel(
    every, hid, own_sum, returned, token_out, down_out, token_v, down_v, sems
):
    planes, local_experts, share, count = hid.shape
    model_width = every.shape[3]
    width = model_width // STEPS
    blocks = width // 128
    stores = []

    def store(src, dst):
        c = pltpu.make_async_copy(src, dst, sems.at[len(stores)])
        c.start()
        stores.append(c)

    pieces = [hid[k].reshape(local_experts * share, count) for k in range(planes)]
    pieces = jnp.concatenate(pieces, axis=1)
    for i in range(STEPS):
        result = jnp.dot(
            pieces,
            every[:, :, :, i * width : (i + 1) * width].reshape(planes * count, width),
            preferred_element_type=jnp.float32,
        )
        lines = down_v.at[i].reshape(share * blocks * local_experts, 128)
        for e in range(local_experts):
            for b in range(blocks):
                lines[pl.ds(b * local_experts + e, share, stride=blocks * local_experts), :] = (
                    result[e * share : (e + 1) * share, b * 128 : (b + 1) * 128]
                )
        store(
            down_v.at[i], down_out.at[:, pl.ds(i * blocks * local_experts, blocks * local_experts)]
        )
        if i == 0:
            total = own_sum[...]
            for d in range(returned.shape[0]):
                total = total + returned[d].astype(jnp.float32)
            token_v[...] = total.astype(jnp.bfloat16)
            store(token_v, token_out)
    for c in stores:
        c.wait()


def fused_shapes(chips, planes, rows, top, local_experts, model_width, hidden_units):
    bf16, f32 = jnp.bfloat16, jnp.float32
    count, width = 2 * chips * rows, model_width // PARTS
    return [
        ((2 * chips, rows, model_width), bf16),
        ((2 * chips, top, rows), jnp.int32),
        ((2 * chips, top, rows), f32),
        ((model_width, 2 * local_experts * hidden_units), bf16),
        ((local_experts * hidden_units, model_width), bf16),
        ((count, 2 * local_experts * hidden_units), f32),
        ((count, local_experts * hidden_units), f32),
        ((local_experts, count, hidden_units), f32),
        ((local_experts, hidden_units, count), bf16),
        ((count, 2 * local_experts * hidden_units), bf16),
        ((PARTS, chips, rows, width), f32),
        ((PARTS, chips, rows, width), bf16),
        ((PARTS, chips, rows, width), bf16),
        ((PARTS, chips, rows, width), bf16),
    ]


def buffer_bytes(shapes):
    total = 0
    for dims, kind in shapes:
        size = jnp.dtype(kind).itemsize
        for dim in dims[:-1]:
            size *= dim
        total += size * (-(-dims[-1] // 128) * 128)
    return total


def plan(tokens, routes, w_gate):
    groups, planes = lax.axis_size("expert"), lax.axis_size("dp")
    chips = groups // 2
    rows, model_width = tokens.shape
    local_experts, _, hidden_units = w_gate.shape
    if groups != 8 or planes != 4:
        return None
    if rows % 16 or hidden_units % 128 or (groups * rows) % 128 or model_width % (128 * PARTS):
        return None
    shapes = fused_shapes(
        chips, planes, rows, routes.shape[1], local_experts, model_width, hidden_units
    )
    passed = planes * groups * rows * model_width * 2
    if buffer_bytes(shapes) > VMEM_BUDGET or passed > VMEM_PASSED:
        return None
    return chips, planes, shapes


def shards(tokens, out_grad, routes, route_gates, w_gate, w_up, w_down):
    planned = plan(tokens, routes, w_gate)
    if planned is None:
        return collective_shards(tokens, out_grad, routes, route_gates, w_gate, w_up, w_down)
    chips, planes, shapes = planned
    rows, model_width = tokens.shape
    local_experts, _, hidden_units = w_gate.shape
    share = hidden_units // planes
    amount = len(copy_keys(chips, planes, local_experts))
    count = 2 * chips * rows
    outside = pl.BlockSpec(memory_space=pltpu.HBM)
    inside = pl.BlockSpec(memory_space=pltpu.VMEM)
    passed = pl.pallas_call(
        functools.partial(fused_kernel, chips, planes),
        out_shape=(
            pltpu.VMEM((planes, 2 * chips, rows, model_width), jnp.bfloat16),
            pltpu.VMEM((planes, local_experts, share, count), jnp.bfloat16),
            pltpu.VMEM((rows, model_width), jnp.float32),
            pltpu.VMEM((chips - 1, rows, model_width), jnp.bfloat16),
        ),
        in_specs=[outside] * 7,
        out_specs=(inside,) * 4,
        scratch_shapes=[pltpu.VMEM(dims, kind) for dims, kind in shapes]
        + [
            pltpu.SemaphoreType.DMA((4 + 5 * local_experts,)),
            pltpu.SemaphoreType.DMA((amount,)),
            pltpu.SemaphoreType.DMA((amount,)),
            pltpu.SemaphoreType.REGULAR,
        ],
        compiler_params=pltpu.CompilerParams(
            collective_id=0, has_side_effects=True, vmem_limit_bytes=VMEM_BUDGET
        ),
        name="expert_backward",
    )(tokens, out_grad, routes.T, route_gates.T, w_gate, w_up, w_down)
    width = model_width // STEPS
    lines = width // 128 * local_experts
    token_grad, down_grad = pl.pallas_call(
        finish_kernel,
        out_shape=(
            jax.ShapeDtypeStruct((rows, model_width), jnp.bfloat16),
            jax.ShapeDtypeStruct((share, model_width // 128 * local_experts, 128), jnp.float32),
        ),
        in_specs=[inside] * 4,
        out_specs=(outside,) * 2,
        scratch_shapes=[
            pltpu.VMEM((rows, model_width), jnp.bfloat16),
            pltpu.VMEM((STEPS, share, lines, 128), jnp.float32),
            pltpu.SemaphoreType.DMA((1 + STEPS,)),
        ],
        compiler_params=pltpu.CompilerParams(vmem_limit_bytes=32 << 20),
        name="expert_finish",
    )(*passed)
    down_grad = down_grad.reshape(share, model_width // 128, local_experts, 128)
    return (token_grad, down_grad.transpose(0, 2, 1, 3).reshape(share, local_experts, model_width))


def solution(mesh):
    placed = (
        P(("expert", "dp"), None),
        P(("expert", "dp"), None),
        P(("expert", "dp"), None),
        P(("expert", "dp"), None),
        P("expert", None, None),
        P("expert", None, None),
        P("expert", None, None),
    )
    return jax.shard_map(
        shards,
        mesh=mesh,
        in_specs=placed,
        out_specs=(P(("expert", "dp"), None), P("dp", "expert", None)),
        check_vma=False,
    )
```

```python
import functools
import math

import jax
import jax.numpy as jnp
from jax import lax
from jax.experimental import pallas as pl
from jax.experimental.pallas import tpu as pltpu
from jax.sharding import PartitionSpec as P

VMEM_BUDGET = 56 << 20
VMEM_PASSED = 4 << 20
STEPS = 2
PARTS = 4
HALVES = 2
ALONG = ((3, 0), (3, 1))
MESH = pl.DeviceIdType.MESH
NT = (((1,), (1,)), ((), ()))


def gate_up(arrived, w_gate, w_up):
    gate_pre = jnp.einsum("erd,edf->erf", arrived, w_gate, preferred_element_type=jnp.float32)
    up_pre = jnp.einsum("erd,edf->erf", arrived, w_up, preferred_element_type=jnp.float32)
    return (gate_pre, up_pre)


def collective_shards(tokens, out_grad, routes, route_gates, w_gate, w_up, w_down):
    tok_count, model_width = tokens.shape
    top_count = routes.shape[1]
    local_experts = w_gate.shape[0]
    groups = lax.axis_size("expert")
    experts = local_experts * groups
    slot_count = 2 * tok_count * top_count // experts
    flat_routes = routes.reshape(-1)
    onehot = (flat_routes[:, None] == jnp.arange(experts, dtype=jnp.int32)[None, :]).astype(
        jnp.int32
    )
    slot_rank = jnp.sum(onehot * (jnp.cumsum(onehot, axis=0) - onehot), axis=1)
    slot_index = flat_routes * slot_count + slot_rank
    placement = slot_index[None, :] == jnp.arange(experts * slot_count, dtype=jnp.int32)[:, None]
    route_place = placement.astype(jnp.bfloat16)
    token_place = jnp.sum(
        placement.reshape(experts * slot_count, tok_count, top_count).astype(jnp.float32), axis=2
    ).astype(jnp.bfloat16)
    send_inputs = (
        jnp.dot(token_place, tokens, preferred_element_type=jnp.float32)
        .astype(jnp.bfloat16)
        .reshape(experts, slot_count, model_width)
    )
    scaled = (
        (route_gates[:, :, None] * out_grad[:, None, :].astype(jnp.float32))
        .astype(jnp.bfloat16)
        .reshape(tok_count * top_count, model_width)
    )
    send_grads = (
        jnp.dot(route_place, scaled, preferred_element_type=jnp.float32)
        .astype(jnp.bfloat16)
        .reshape(experts, slot_count, model_width)
    )
    arrived, arrived_grad = (
        lax.all_to_all(send_inputs, "expert", split_axis=0, concat_axis=1, tiled=True),
        lax.all_to_all(send_grads, "expert", split_axis=0, concat_axis=1, tiled=True),
    )
    gate_pre, up_pre = gate_up(arrived, w_gate, w_up)
    sigmoid_gate = jax.nn.sigmoid(gate_pre)
    silu_gate = gate_pre * sigmoid_gate
    hidden = (silu_gate * up_pre).astype(jnp.bfloat16)
    hidden_grad = jnp.einsum(
        "erd,efd->erf", arrived_grad, w_down, preferred_element_type=jnp.float32
    )
    gate_grad = (
        hidden_grad * up_pre * (sigmoid_gate + gate_pre * sigmoid_gate * (1.0 - sigmoid_gate))
    ).astype(jnp.bfloat16)
    up_grad = (hidden_grad * silu_gate).astype(jnp.bfloat16)
    row_grads = (
        jnp.einsum("erf,edf->erd", gate_grad, w_gate, preferred_element_type=jnp.float32)
        + jnp.einsum("erf,edf->erd", up_grad, w_up, preferred_element_type=jnp.float32)
    ).astype(jnp.bfloat16)
    returned = lax.all_to_all(row_grads, "expert", split_axis=1, concat_axis=0, tiled=True)
    token_grad = lax.dot_general(
        token_place,
        returned.reshape(experts * slot_count, model_width),
        (((0,), (0,)), ((), ())),
        preferred_element_type=jnp.float32,
    ).astype(jnp.bfloat16)
    hidden_units = hidden.shape[2]
    share_rows = hidden_units // lax.axis_size("dp")
    partial_grad = jnp.einsum(
        "erf,erd->fed", hidden, arrived_grad, preferred_element_type=jnp.float32
    ).astype(jnp.bfloat16)
    total_grad = lax.psum(partial_grad, "dp").astype(jnp.float32)
    first_row = lax.axis_index("dp") * share_rows
    down_grad = lax.dynamic_slice_in_dim(total_grad, first_row, share_rows, 0)
    return (token_grad, down_grad)


def flip(index, bits):
    out, step = index, 1
    while step <= bits:
        if bits & step:
            out = out + step * (1 - 2 * ((index // step) % 2))
        step *= 2
    return out


def arrival_groups(planes):
    names = ["r", "g", "rc", "gc", "h", "t"]
    names += [("z", k) for k in range(1, planes)]
    for lead in [("x",)] + [("d", k) for k in range(planes)]:
        names += [lead + (1, 0), lead + (2, 1), lead + ("rest",), lead + (3,)]
    names += [(name, h) for name in ("xc", "dc") for h in range(HALVES)]
    names += [("dk", k) for k in range(1, planes)] + [("p", j) for j in range(PARTS)]
    return {name: i for i, name in enumerate(names)}


def group_of(key):
    name = key[0]
    if name in ("z", "p"):
        return key
    if name in ("r", "g", "rc", "gc", "h", "t"):
        return name
    if name in ("xc", "dc"):
        return (name, key[2])
    if name == "dk":
        return key[:2]
    d, h = key[-2:]
    lead = key[:-2]
    if d == 3:
        return lead + (3,)
    return lead + ((d, h) if (d, h) in ((1, 0), (2, 1)) else ("rest",))


def fused_kernel(
    chips, planes, tok, dy, rt, gt, wg, wu, wd, every, hid_in, own_sum, ret_in,
    xb, rb, gb, wide, wdv, pre, grads, hid_f, hid_out, both,
    keep, pair_out, pair_in, ret_out, lsem, ssem, rsem, known,
):
    local_experts, model_width, hidden_units = wg.shape
    rows = tok.shape[0]
    count = 2 * chips * rows
    share = hidden_units // planes
    width = model_width // PARTS
    half = model_width // HALVES
    me, plane = lax.axis_index("expert"), lax.axis_index("dp")
    chip, core = me // 2, me % 2
    inner = (plane % 2) != (plane // 2)
    partner = {"expert": chip * 2 + 1 - core, "dp": plane}
    across = [{"expert": flip(chip, d) * 2 + core, "dp": plane} for d in range(chips)]
    above = [{"expert": me, "dp": flip(plane, k)} for k in range(planes)]
    groups = arrival_groups(planes)

    def load(src, dst, i):
        c = pltpu.make_async_copy(src, dst, lsem.at[i])
        c.start()
        return c

    own = [
        load(src, dst, i)
        for i, (src, dst) in enumerate(
            ((dy, every.at[0, 0]), (tok, xb.at[0]), (rt, rb.at[0]), (gt, gb.at[0]))
        )
    ]

    def load_weights():
        load(wd, wdv, 4)
        for e in range(local_experts):
            for i, w in enumerate((wg, wu)):
                load(w.at[e], wide.at[:, pl.ds((2 * e + i) * hidden_units, hidden_units)], 5)

    def remote(key, src, dst, target):
        return pltpu.make_async_remote_copy(
            src_ref=src, dst_ref=dst, send_sem=ssem.at[{"r": 1, "g": 2}.get(key[0][0], 0)],
            recv_sem=rsem.at[groups[group_of(key)]], device_id=target, device_id_type=MESH,
        )

    def whole(ref, sem):
        pltpu.make_async_copy(ref, ref, sem).wait()

    def cols(h):
        return pl.ds(h * half, half)

    copies = {}
    for name, src, buf in (("r", rt, rb), ("g", gt, gb)):
        for d in range(chips):
            if d:
                copies[name, d] = remote((name, d), src, buf.at[2 * d], across[d])
            copies[name + "c", d] = remote(
                (name + "c", d), buf.at[2 * d] if d else src, buf.at[2 * d + 1], partner
            )

    def spread(name, first, buf, lead):
        for h in range(HALVES):
            for d in (1, 2):
                copies[(name,) + lead + (d, h)] = remote(
                    (name,) + lead + (d, h), first.at[:, cols(h)], buf.at[2 * d, :, cols(h)], across[d]
                )
            if lead == (1,) and (3, h) in ALONG:
                continue
            via, to = (1, 2) if h == 0 else (2, 1)
            copies[(name,) + lead + (3, h)] = remote(
                (name,) + lead + (3, h), buf.at[2 * via, :, cols(h)], buf.at[6, :, cols(h)], across[to]
            )

    spread("x", tok, xb, ())
    for d in range(chips):
        for h in range(HALVES):
            for key, first, buf in ((("xc",), tok, xb), (("dc",), dy, every.at[0])):
                copies[key + (d, h)] = remote(
                    key + (d, h),
                    buf.at[2 * d, :, cols(h)] if d else first.at[:, cols(h)],
                    buf.at[2 * d + 1, :, cols(h)],
                    partner,
                )
    for k in range(planes):
        spread("d", every.at[k, 0] if k else dy, every.at[k], (k,))
        if k:
            for d in range(chips):
                copies["dk", k, d] = remote(
                    ("dk", k, d), every.at[k, 2 * d], every.at[k, 2 * d + 1], partner
                )
            copies["z", k] = remote(("z", k), dy, every.at[k, 0], above[k])
    for d, h in ALONG:
        copies["d", 1, d, h] = remote(
            ("d", 1, d, h), every.at[0, 2 * d, :, cols(h)], every.at[1, 2 * d, :, cols(h)], above[1]
        )
    for k in range(1, planes):
        first = pl.multiple_of(flip(plane, k) * share, 16)
        for e in range(local_experts):
            copies["h", k, e] = remote(
                ("h", k, e), hid_out.at[e, pl.ds(first, share)], hid_in.at[k, e], above[k]
            )
    for j in range(PARTS):
        copies["p", j] = remote(("p", j), pair_out.at[j], pair_in.at[j], partner)
        for d in range(1, chips):
            copies["t", j, d] = remote(
                ("t", j, d), ret_out.at[j, d], ret_in.at[d - 1, :, pl.ds(j * width, width)], across[d]
            )

    def start(*key):
        copies[key].start()

    def arrive(group, ref):
        whole(ref, rsem.at[groups[group]])

    def place(lead):
        return xb if lead == ("x",) else every.at[lead[1]]

    def relay(*lead):
        for d, h in ((1, 0), (2, 1)):
            arrive(lead + (d, h), place(lead).at[2 * d, :, cols(h)])
            if lead != ("d", 1) or (3, h) not in ALONG:
                start(*lead, 3, h)
            if lead in (("x",), ("d", 0)):
                start(lead[0] + "c", d, h)

    def rest(*lead):
        arrive(lead + ("rest",), place(lead).at[2])
        for d, h in ((1, 1), (2, 0)):
            if lead in (("x",), ("d", 0)):
                start(lead[0] + "c", d, h)
            else:
                start("dk", lead[1], d)

    def diagonal_in(*lead):
        arrive(lead + (3,), place(lead).at[6])
        if lead in (("x",), ("d", 0)):
            for h in range(HALVES):
                start(lead[0] + "c", 3, h)
        else:
            start("dk", lead[1], 3)

    def plane_in(k):
        arrive(("z", k), every.at[k, 0])
        for h in range(HALVES):
            for d in (1, 2):
                start("d", k, d, h if d == 1 else 1 - h)
        start("dk", k, 0)

    barrier = pltpu.get_barrier_semaphore()
    for target in [partner] + across[1:3] + [above[1]]:
        pl.semaphore_signal(barrier, inc=1, device_id=target, device_id_type=MESH)

    @pl.when(inner)
    def _():
        pl.semaphore_signal(barrier, inc=1, device_id=above[3], device_id_type=MESH)

    pl.semaphore_wait(barrier, 4 + inner.astype(jnp.int32))

    @pl.when(inner)
    def _():
        pl.semaphore_signal(known, inc=1, device_id=above[3], device_id_type=MESH)
        copies["z", 3].start()

    for h in range(HALVES):
        for d in (1, 2):
            start("d", 0, d, h if d == 1 else 1 - h)
    start("z", 1)
    for h in range(HALVES):
        start("dc", 0, h)
    for name in ("r", "g"):
        for d in (1, 2):
            start(name, d)
        start(name + "c", 0)
    for h in range(HALVES):
        for d in (1, 2):
            start("x", d, h if d == 1 else 1 - h)
        start("xc", 0, h)
    load_weights()

    @pl.when(inner)
    def _():
        pl.semaphore_wait(known, 1)
        pl.semaphore_signal(known, inc=1, device_id=above[1], device_id_type=MESH)
        copies["z", 2].start()

    relay("d", 0)
    rest("d", 0)
    for name in ("r", "g"):
        start(name, 3)

    @pl.when(jnp.logical_not(inner))
    def _():
        pl.semaphore_wait(known, 1)
        copies["z", 3].start()
        copies["z", 2].start()

    relay("x")
    rest("x")
    for c in own:
        c.wait()
    plane_in(1)
    diagonal_in("d", 0)
    for d, h in ALONG:
        start("d", 1, d, h)
    plane_in(2)
    diagonal_in("x")
    for name, buf in (("r", rb), ("g", gb)):
        arrive(name, buf.at[pl.ds(0, chips - 1)])
        for d in range(1, chips):
            start(name + "c", d)
    plane_in(3)

    whole(wdv, lsem.at[4])
    for h in range(HALVES):
        arrive(("dc", h), every.at[0, pl.ds(0, chips), :, cols(h)])
        begin = h * half
        term = lax.dot_general(
            wdv[:, :, begin : begin + half].reshape(local_experts * hidden_units, half),
            every[0, :, :, begin : begin + half].reshape(count, half),
            NT,
            preferred_element_type=jnp.float32,
        ).T
        grads[...] = grads[...] + term if h else term
    whole(wide, lsem.at[5])
    for h in range(HALVES):
        arrive(("xc", h), xb.at[pl.ds(0, chips), :, cols(h)])
        begin = h * half
        term = jnp.dot(
            xb[:, :, begin : begin + half].reshape(count, half),
            wide[begin : begin + half, :],
            preferred_element_type=jnp.float32,
        )
        pre[...] = pre[...] + term if h else term
        if h == 0:
            relay("d", 1)
    rest("d", 1)
    arrive("rc", rb.at[pl.ds(0, chips)])
    arrive("gc", gb.at[pl.ds(0, chips)])

    named, given = rb[...], gb[...]
    diagonal = lax.broadcasted_iota(jnp.int32, (1, rows, rows), 1) == lax.broadcasted_iota(
        jnp.int32, (1, rows, rows), 2
    )
    for e in range(local_experts):
        gain = jnp.sum(
            jnp.where(named == me * local_experts + e, given, 0.0), axis=1, keepdims=True
        )
        gain = jnp.sum(jnp.where(diagonal, gain, 0.0), axis=2, keepdims=True).reshape(count, 1)
        a, b, c = ((2 * e + i) * hidden_units for i in range(3))
        hidden_grad = gain * grads[:, e * hidden_units : (e + 1) * hidden_units]
        gate_pre, up_pre = pre[:, a:b], pre[:, b:c]
        s = jax.nn.sigmoid(gate_pre)
        silu = gate_pre * s
        hid_f[e] = silu * up_pre * gain
        both[:, a:b] = (hidden_grad * up_pre * (s + gate_pre * s * (1.0 - s))).astype(jnp.bfloat16)
        both[:, b:c] = (hidden_grad * silu).astype(jnp.bfloat16)

    for j in range(PARTS + 1):
        if j < PARTS:
            total = lax.dot_general(
                wide[j * width : (j + 1) * width, :], both[...], NT, preferred_element_type=jnp.float32
            ).T.reshape(chips, 2, rows, width)
            pair_out[j] = total[:, 1].astype(jnp.bfloat16)
            start("p", j)
            keep[j] = total[:, 0]
        if j == 0:
            relay("d", 2)
        if j == 1:
            for e in range(local_experts):
                hid_out[e] = hid_f[e].T.astype(jnp.bfloat16)
            for k in range(1, planes):
                for e in range(local_experts):
                    start("h", k, e)
            first = pl.multiple_of(plane * share, 16)
            for e in range(local_experts):
                load(hid_out.at[e, pl.ds(first, share)], hid_in.at[0, e], 6)
            relay("d", 3)
        if j == 2:
            rest("d", 2)
            diagonal_in("d", 1)
        if j == 3:
            rest("d", 3)
        if j:
            i = j - 1
            arrive(("p", i), pair_in.at[i])
            total = keep[i] + pair_in[i].astype(jnp.float32)
            for d in range(chips - 1, 0, -1):
                ret_out[i, d] = total[d].astype(jnp.bfloat16)
            for d in range(chips - 1, 0, -1):
                start("t", i, d)
            own_sum[:, i * width : (i + 1) * width] = total[0]

    diagonal_in("d", 2)
    diagonal_in("d", 3)
    arrive("h", hid_in.at[pl.ds(1, planes - 1)])
    for k in range(1, planes):
        arrive(("dk", k), every.at[k, pl.ds(0, chips)])
    arrive("t", ret_in)
    whole(hid_in.at[0], lsem.at[6])
    sent = sum(
        math.prod(c.src_ref.shape) for key, c in copies.items() if key[0][0] not in ("r", "g")
    )
    whole(wide.at[pl.ds(0, sent // wide.shape[1])], ssem.at[0])
    for i, buf in ((1, rb), (2, gb)):
        whole(buf.at[pl.ds(0, 2 * chips - 1)], ssem.at[i])


def finish_kernel(
    every, hid, own_sum, returned, token_out, down_out, token_v, down_v, sems
):
    planes, local_experts, share, count = hid.shape
    model_width = every.shape[3]
    width = model_width // STEPS
    blocks = width // 128
    stores = []

    def store(src, dst):
        c = pltpu.make_async_copy(src, dst, sems.at[len(stores)])
        c.start()
        stores.append(c)

    pieces = [hid[k].reshape(local_experts * share, count) for k in range(planes)]
    pieces = jnp.concatenate(pieces, axis=1)
    for i in range(STEPS):
        result = jnp.dot(
            pieces,
            every[:, :, :, i * width : (i + 1) * width].reshape(planes * count, width),
            preferred_element_type=jnp.float32,
        )
        lines = down_v.at[i].reshape(share * blocks * local_experts, 128)
        for e in range(local_experts):
            for b in range(blocks):
                lines[pl.ds(b * local_experts + e, share, stride=blocks * local_experts), :] = (
                    result[e * share : (e + 1) * share, b * 128 : (b + 1) * 128]
                )
        store(
            down_v.at[i], down_out.at[:, pl.ds(i * blocks * local_experts, blocks * local_experts)]
        )
        if i == 0:
            total = own_sum[...]
            for d in range(returned.shape[0]):
                total = total + returned[d].astype(jnp.float32)
            token_v[...] = total.astype(jnp.bfloat16)
            store(token_v, token_out)
    for c in stores:
        c.wait()


def fused_shapes(chips, planes, rows, top, local_experts, model_width, hidden_units):
    bf16, f32 = jnp.bfloat16, jnp.float32
    count, width = 2 * chips * rows, model_width // PARTS
    return [
        ((2 * chips, rows, model_width), bf16),
        ((2 * chips, top, rows), jnp.int32),
        ((2 * chips, top, rows), f32),
        ((model_width, 2 * local_experts * hidden_units), bf16),
        ((local_experts, hidden_units, model_width), bf16),
        ((count, 2 * local_experts * hidden_units), f32),
        ((count, local_experts * hidden_units), f32),
        ((local_experts, count, hidden_units), f32),
        ((local_experts, hidden_units, count), bf16),
        ((count, 2 * local_experts * hidden_units), bf16),
        ((PARTS, chips, rows, width), f32),
        ((PARTS, chips, rows, width), bf16),
        ((PARTS, chips, rows, width), bf16),
        ((PARTS, chips, rows, width), bf16),
    ]


def buffer_bytes(shapes):
    total = 0
    for dims, kind in shapes:
        size = jnp.dtype(kind).itemsize
        for dim in dims[:-1]:
            size *= dim
        total += size * (-(-dims[-1] // 128) * 128)
    return total


def plan(tokens, routes, w_gate):
    groups, planes = lax.axis_size("expert"), lax.axis_size("dp")
    chips = groups // 2
    rows, model_width = tokens.shape
    local_experts, _, hidden_units = w_gate.shape
    if groups != 8 or planes != 4:
        return None
    if rows % 16 or hidden_units % 128 or (groups * rows) % 128 or model_width % (128 * PARTS):
        return None
    shapes = fused_shapes(
        chips, planes, rows, routes.shape[1], local_experts, model_width, hidden_units
    )
    passed = planes * groups * rows * model_width * 2
    if buffer_bytes(shapes) > VMEM_BUDGET or passed > VMEM_PASSED:
        return None
    return chips, planes, shapes


def shards(tokens, out_grad, routes, route_gates, w_gate, w_up, w_down):
    planned = plan(tokens, routes, w_gate)
    if planned is None:
        return collective_shards(tokens, out_grad, routes, route_gates, w_gate, w_up, w_down)
    chips, planes, shapes = planned
    rows, model_width = tokens.shape
    local_experts, _, hidden_units = w_gate.shape
    share = hidden_units // planes
    amount = len(arrival_groups(planes))
    count = 2 * chips * rows
    outside = pl.BlockSpec(memory_space=pltpu.HBM)
    inside = pl.BlockSpec(memory_space=pltpu.VMEM)
    passed = pl.pallas_call(
        functools.partial(fused_kernel, chips, planes),
        out_shape=(
            pltpu.VMEM((planes, 2 * chips, rows, model_width), jnp.bfloat16),
            pltpu.VMEM((planes, local_experts, share, count), jnp.bfloat16),
            pltpu.VMEM((rows, model_width), jnp.float32),
            pltpu.VMEM((chips - 1, rows, model_width), jnp.bfloat16),
        ),
        in_specs=[outside] * 7,
        out_specs=(inside,) * 4,
        scratch_shapes=[pltpu.VMEM(dims, kind) for dims, kind in shapes]
        + [
            pltpu.SemaphoreType.DMA((7,)),
            pltpu.SemaphoreType.DMA((3,)),
            pltpu.SemaphoreType.DMA((amount,)),
            pltpu.SemaphoreType.REGULAR,
        ],
        compiler_params=pltpu.CompilerParams(
            collective_id=0, has_side_effects=True, vmem_limit_bytes=VMEM_BUDGET
        ),
        name="expert_backward",
    )(tokens, out_grad, routes.T, route_gates.T, w_gate, w_up, w_down)
    width = model_width // STEPS
    lines = width // 128 * local_experts
    token_grad, down_grad = pl.pallas_call(
        finish_kernel,
        out_shape=(
            jax.ShapeDtypeStruct((rows, model_width), jnp.bfloat16),
            jax.ShapeDtypeStruct((share, model_width // 128 * local_experts, 128), jnp.float32),
        ),
        in_specs=[inside] * 4,
        out_specs=(outside,) * 2,
        scratch_shapes=[
            pltpu.VMEM((rows, model_width), jnp.bfloat16),
            pltpu.VMEM((STEPS, share, lines, 128), jnp.float32),
            pltpu.SemaphoreType.DMA((1 + STEPS,)),
        ],
        compiler_params=pltpu.CompilerParams(vmem_limit_bytes=32 << 20),
        name="expert_finish",
    )(*passed)
    down_grad = down_grad.reshape(share, model_width // 128, local_experts, 128)
    return (token_grad, down_grad.transpose(0, 2, 1, 3).reshape(share, local_experts, model_width))


def solution(mesh):
    placed = (
        P(("expert", "dp"), None),
        P(("expert", "dp"), None),
        P(("expert", "dp"), None),
        P(("expert", "dp"), None),
        P("expert", None, None),
        P("expert", None, None),
        P("expert", None, None),
    )
    return jax.shard_map(
        shards,
        mesh=mesh,
        in_specs=placed,
        out_specs=(P(("expert", "dp"), None), P("dp", "expert", None)),
        check_vma=False,
    )
```

```python
import functools
import math

import jax
import jax.numpy as jnp
from jax import lax
from jax.experimental import pallas as pl
from jax.experimental.pallas import tpu as pltpu
from jax.sharding import PartitionSpec as P

VMEM_BUDGET = 56 << 20
VMEM_PASSED = 4 << 20
STEPS = 2
PARTS = 4
HALVES = 2
ALONG = ((3, 0), (3, 1))
MESH = pl.DeviceIdType.MESH
NT = (((1,), (1,)), ((), ()))


def gate_up(arrived, w_gate, w_up):
    gate_pre = jnp.einsum("erd,edf->erf", arrived, w_gate, preferred_element_type=jnp.float32)
    up_pre = jnp.einsum("erd,edf->erf", arrived, w_up, preferred_element_type=jnp.float32)
    return (gate_pre, up_pre)


def collective_shards(tokens, out_grad, routes, route_gates, w_gate, w_up, w_down):
    tok_count, model_width = tokens.shape
    top_count = routes.shape[1]
    local_experts = w_gate.shape[0]
    groups = lax.axis_size("expert")
    experts = local_experts * groups
    slot_count = 2 * tok_count * top_count // experts
    flat_routes = routes.reshape(-1)
    onehot = (flat_routes[:, None] == jnp.arange(experts, dtype=jnp.int32)[None, :]).astype(
        jnp.int32
    )
    slot_rank = jnp.sum(onehot * (jnp.cumsum(onehot, axis=0) - onehot), axis=1)
    slot_index = flat_routes * slot_count + slot_rank
    placement = slot_index[None, :] == jnp.arange(experts * slot_count, dtype=jnp.int32)[:, None]
    route_place = placement.astype(jnp.bfloat16)
    token_place = jnp.sum(
        placement.reshape(experts * slot_count, tok_count, top_count).astype(jnp.float32), axis=2
    ).astype(jnp.bfloat16)
    send_inputs = (
        jnp.dot(token_place, tokens, preferred_element_type=jnp.float32)
        .astype(jnp.bfloat16)
        .reshape(experts, slot_count, model_width)
    )
    scaled = (
        (route_gates[:, :, None] * out_grad[:, None, :].astype(jnp.float32))
        .astype(jnp.bfloat16)
        .reshape(tok_count * top_count, model_width)
    )
    send_grads = (
        jnp.dot(route_place, scaled, preferred_element_type=jnp.float32)
        .astype(jnp.bfloat16)
        .reshape(experts, slot_count, model_width)
    )
    arrived, arrived_grad = (
        lax.all_to_all(send_inputs, "expert", split_axis=0, concat_axis=1, tiled=True),
        lax.all_to_all(send_grads, "expert", split_axis=0, concat_axis=1, tiled=True),
    )
    gate_pre, up_pre = gate_up(arrived, w_gate, w_up)
    sigmoid_gate = jax.nn.sigmoid(gate_pre)
    silu_gate = gate_pre * sigmoid_gate
    hidden = (silu_gate * up_pre).astype(jnp.bfloat16)
    hidden_grad = jnp.einsum(
        "erd,efd->erf", arrived_grad, w_down, preferred_element_type=jnp.float32
    )
    gate_grad = (
        hidden_grad * up_pre * (sigmoid_gate + gate_pre * sigmoid_gate * (1.0 - sigmoid_gate))
    ).astype(jnp.bfloat16)
    up_grad = (hidden_grad * silu_gate).astype(jnp.bfloat16)
    row_grads = (
        jnp.einsum("erf,edf->erd", gate_grad, w_gate, preferred_element_type=jnp.float32)
        + jnp.einsum("erf,edf->erd", up_grad, w_up, preferred_element_type=jnp.float32)
    ).astype(jnp.bfloat16)
    returned = lax.all_to_all(row_grads, "expert", split_axis=1, concat_axis=0, tiled=True)
    token_grad = lax.dot_general(
        token_place,
        returned.reshape(experts * slot_count, model_width),
        (((0,), (0,)), ((), ())),
        preferred_element_type=jnp.float32,
    ).astype(jnp.bfloat16)
    hidden_units = hidden.shape[2]
    share_rows = hidden_units // lax.axis_size("dp")
    partial_grad = jnp.einsum(
        "erf,erd->fed", hidden, arrived_grad, preferred_element_type=jnp.float32
    ).astype(jnp.bfloat16)
    total_grad = lax.psum(partial_grad, "dp").astype(jnp.float32)
    first_row = lax.axis_index("dp") * share_rows
    down_grad = lax.dynamic_slice_in_dim(total_grad, first_row, share_rows, 0)
    return (token_grad, down_grad)


def flip(index, bits):
    out, step = index, 1
    while step <= bits:
        if bits & step:
            out = out + step * (1 - 2 * ((index // step) % 2))
        step *= 2
    return out


def arrival_groups(planes):
    names = ["r", "g", "rc", "gc", "h", "t"]
    names += [("z", k) for k in range(1, planes)]
    for lead in [("x",)] + [("d", k) for k in range(planes)]:
        names += [lead + (1, 0), lead + (2, 1), lead + ("rest",), lead + (3,)]
    names += [(name, h) for name in ("xc", "dc") for h in range(HALVES)]
    names += [("dk", k) for k in range(1, planes)] + [("p", j) for j in range(PARTS)]
    return {name: i for i, name in enumerate(names)}


def group_of(key):
    name = key[0]
    if name in ("z", "p"):
        return key
    if name in ("r", "g", "rc", "gc", "h", "t"):
        return name
    if name in ("xc", "dc"):
        return (name, key[2])
    if name == "dk":
        return key[:2]
    d, h = key[-2:]
    lead = key[:-2]
    if d == 3:
        return lead + (3,)
    return lead + ((d, h) if (d, h) in ((1, 0), (2, 1)) else ("rest",))


def fused_kernel(
    chips, planes, tok, dy, rt, gt, wg, wu, wd, down_v, own_sum, ret_in,
    every, hid_in, xb, rb, gb, wide, wdv, pre, grads, hid_out, both,
    keep, pair_out, pair_in, ret_out, lsem, ssem, rsem, known,
):
    local_experts, model_width, hidden_units = wg.shape
    rows = tok.shape[0]
    count = 2 * chips * rows
    share = hidden_units // planes
    width = model_width // PARTS
    half = model_width // HALVES
    me, plane = lax.axis_index("expert"), lax.axis_index("dp")
    chip, core = me // 2, me % 2
    inner = (plane % 2) != (plane // 2)
    partner = {"expert": chip * 2 + 1 - core, "dp": plane}
    across = [{"expert": flip(chip, d) * 2 + core, "dp": plane} for d in range(chips)]
    above = [{"expert": me, "dp": flip(plane, k)} for k in range(planes)]
    groups = arrival_groups(planes)

    def load(src, dst, i):
        c = pltpu.make_async_copy(src, dst, lsem.at[i])
        c.start()
        return c

    own = [
        load(src, dst, i)
        for i, (src, dst) in enumerate(
            ((dy, every.at[0, 0]), (tok, xb.at[0]), (rt, rb.at[0]), (gt, gb.at[0]))
        )
    ]

    def load_weights():
        load(wd, wdv, 4)
        for e in range(local_experts):
            for i, w in enumerate((wg, wu)):
                load(w.at[e], wide.at[:, pl.ds((2 * e + i) * hidden_units, hidden_units)], 5)

    def remote(key, src, dst, target):
        return pltpu.make_async_remote_copy(
            src_ref=src, dst_ref=dst, send_sem=ssem.at[{"r": 1, "g": 2}.get(key[0][0], 0)],
            recv_sem=rsem.at[groups[group_of(key)]], device_id=target, device_id_type=MESH,
        )

    def whole(ref, sem):
        pltpu.make_async_copy(ref, ref, sem).wait()

    def cols(h):
        return pl.ds(h * half, half)

    copies = {}
    for name, src, buf in (("r", rt, rb), ("g", gt, gb)):
        for d in range(chips):
            if d:
                copies[name, d] = remote((name, d), src, buf.at[2 * d], across[d])
            copies[name + "c", d] = remote(
                (name + "c", d), buf.at[2 * d] if d else src, buf.at[2 * d + 1], partner
            )

    def spread(name, first, buf, lead):
        for h in range(HALVES):
            for d in (1, 2):
                copies[(name,) + lead + (d, h)] = remote(
                    (name,) + lead + (d, h), first.at[:, cols(h)], buf.at[2 * d, :, cols(h)], across[d]
                )
            if lead == (1,) and (3, h) in ALONG:
                continue
            via, to = (1, 2) if h == 0 else (2, 1)
            copies[(name,) + lead + (3, h)] = remote(
                (name,) + lead + (3, h), buf.at[2 * via, :, cols(h)], buf.at[6, :, cols(h)], across[to]
            )

    spread("x", tok, xb, ())
    for d in range(chips):
        for h in range(HALVES):
            for key, first, buf in ((("xc",), tok, xb), (("dc",), dy, every.at[0])):
                copies[key + (d, h)] = remote(
                    key + (d, h),
                    buf.at[2 * d, :, cols(h)] if d else first.at[:, cols(h)],
                    buf.at[2 * d + 1, :, cols(h)],
                    partner,
                )
    for k in range(planes):
        spread("d", every.at[k, 0] if k else dy, every.at[k], (k,))
        if k:
            for d in range(chips):
                copies["dk", k, d] = remote(
                    ("dk", k, d), every.at[k, 2 * d], every.at[k, 2 * d + 1], partner
                )
            copies["z", k] = remote(("z", k), dy, every.at[k, 0], above[k])
    for d, h in ALONG:
        copies["d", 1, d, h] = remote(
            ("d", 1, d, h), every.at[0, 2 * d, :, cols(h)], every.at[1, 2 * d, :, cols(h)], above[1]
        )
    for k in range(1, planes):
        first = pl.multiple_of(flip(plane, k) * share, 16)
        for e in range(local_experts):
            copies["h", k, e] = remote(
                ("h", k, e), hid_out.at[e, pl.ds(first, share)], hid_in.at[k, e], above[k]
            )
    for j in range(PARTS):
        copies["p", j] = remote(("p", j), pair_out.at[j], pair_in.at[j], partner)
        for d in range(1, chips):
            copies["t", j, d] = remote(
                ("t", j, d), ret_out.at[j, d], ret_in.at[d - 1, :, pl.ds(j * width, width)], across[d]
            )

    def start(*key):
        copies[key].start()

    def arrive(group, ref):
        whole(ref, rsem.at[groups[group]])

    def place(lead):
        return xb if lead == ("x",) else every.at[lead[1]]

    def relay(*lead):
        for d, h in ((1, 0), (2, 1)):
            arrive(lead + (d, h), place(lead).at[2 * d, :, cols(h)])
            if lead != ("d", 1) or (3, h) not in ALONG:
                start(*lead, 3, h)
            if lead in (("x",), ("d", 0)):
                start(lead[0] + "c", d, h)

    def rest(*lead):
        arrive(lead + ("rest",), place(lead).at[2])
        for d, h in ((1, 1), (2, 0)):
            if lead in (("x",), ("d", 0)):
                start(lead[0] + "c", d, h)
            else:
                start("dk", lead[1], d)

    def diagonal_in(*lead):
        arrive(lead + (3,), place(lead).at[6])
        if lead in (("x",), ("d", 0)):
            for h in range(HALVES):
                start(lead[0] + "c", 3, h)
        else:
            start("dk", lead[1], 3)

    def plane_in(k):
        arrive(("z", k), every.at[k, 0])
        for h in range(HALVES):
            for d in (1, 2):
                start("d", k, d, h if d == 1 else 1 - h)
        start("dk", k, 0)

    barrier = pltpu.get_barrier_semaphore()
    for target in [partner] + across[1:3] + [above[1]]:
        pl.semaphore_signal(barrier, inc=1, device_id=target, device_id_type=MESH)

    @pl.when(inner)
    def _():
        pl.semaphore_signal(barrier, inc=1, device_id=above[3], device_id_type=MESH)

    pl.semaphore_wait(barrier, 4 + inner.astype(jnp.int32))

    @pl.when(inner)
    def _():
        pl.semaphore_signal(known, inc=1, device_id=above[3], device_id_type=MESH)
        copies["z", 3].start()

    for h in range(HALVES):
        for d in (1, 2):
            start("d", 0, d, h if d == 1 else 1 - h)
    start("z", 1)
    for h in range(HALVES):
        start("dc", 0, h)
    for name in ("r", "g"):
        for d in (1, 2):
            start(name, d)
        start(name + "c", 0)
    for h in range(HALVES):
        for d in (1, 2):
            start("x", d, h if d == 1 else 1 - h)
        start("xc", 0, h)
    load_weights()

    @pl.when(inner)
    def _():
        pl.semaphore_wait(known, 1)
        pl.semaphore_signal(known, inc=1, device_id=above[1], device_id_type=MESH)
        copies["z", 2].start()

    @pl.when(jnp.logical_not(inner))
    def _():
        pl.semaphore_wait(known, 1)
        copies["z", 3].start()
        copies["z", 2].start()

    relay("d", 0)
    rest("d", 0)
    for name in ("r", "g"):
        start(name, 3)

    relay("x")
    rest("x")
    for c in own:
        c.wait()
    diagonal_in("d", 0)
    for d, h in ALONG:
        start("d", 1, d, h)
    plane_in(1)
    diagonal_in("x")
    for name, buf in (("r", rb), ("g", gb)):
        arrive(name, buf.at[pl.ds(0, chips - 1)])
        for d in range(1, chips):
            start(name + "c", d)
    plane_in(2)

    whole(wdv, lsem.at[4])
    for h in range(HALVES):
        arrive(("dc", h), every.at[0, pl.ds(0, chips), :, cols(h)])
        begin = h * half
        term = lax.dot_general(
            every[0, :, :, begin : begin + half].reshape(count, half),
            wdv[:, :, begin : begin + half].reshape(local_experts * hidden_units, half),
            NT,
            preferred_element_type=jnp.float32,
        )
        grads[...] = grads[...] + term if h else term
    whole(wide, lsem.at[5])
    plane_in(3)
    for h in range(HALVES):
        arrive(("xc", h), xb.at[pl.ds(0, chips), :, cols(h)])
        begin = h * half
        term = jnp.dot(
            xb[:, :, begin : begin + half].reshape(count, half),
            wide[begin : begin + half, :],
            preferred_element_type=jnp.float32,
        )
        pre[...] = pre[...] + term if h else term
    relay("d", 1)
    rest("d", 1)
    arrive("rc", rb.at[pl.ds(0, chips)])
    arrive("gc", gb.at[pl.ds(0, chips)])

    named, given = rb[...], gb[...]
    diagonal = lax.broadcasted_iota(jnp.int32, (1, rows, rows), 1) == lax.broadcasted_iota(
        jnp.int32, (1, rows, rows), 2
    )
    for e in range(local_experts):
        gain = jnp.sum(
            jnp.where(named == me * local_experts + e, given, 0.0), axis=1, keepdims=True
        )
        gain = jnp.sum(jnp.where(diagonal, gain, 0.0), axis=2, keepdims=True).reshape(count, 1)
        a, b, c = ((2 * e + i) * hidden_units for i in range(3))
        hidden_grad = gain * grads[:, e * hidden_units : (e + 1) * hidden_units]
        gate_pre, up_pre = pre[:, a:b], pre[:, b:c]
        s = jax.nn.sigmoid(gate_pre)
        silu = gate_pre * s
        hid_out[e] = (silu * up_pre * gain).T.astype(jnp.bfloat16)
        both[:, a:b] = (hidden_grad * up_pre * (s + gate_pre * s * (1.0 - s))).astype(jnp.bfloat16)
        both[:, b:c] = (hidden_grad * silu).astype(jnp.bfloat16)

    for k in range(planes - 1, 0, -1):
        for e in range(local_experts):
            start("h", k, e)
    first = pl.multiple_of(plane * share, 16)
    for e in range(local_experts):
        load(hid_out.at[e, pl.ds(first, share)], hid_in.at[0, e], 6)

    for j in range(PARTS + 1):
        if j < PARTS:
            total = lax.dot_general(
                both[...], wide[j * width : (j + 1) * width, :], NT, preferred_element_type=jnp.float32
            ).reshape(chips, 2, rows, width)
            pair_out[j] = total[:, 1].astype(jnp.bfloat16)
            start("p", j)
            keep[j] = total[:, 0]
        if j == 0:
            relay("d", 2)
        if j == 2:
            relay("d", 3)
            rest("d", 2)
        if j == 3:
            rest("d", 3)
        if j:
            i = j - 1
            arrive(("p", i), pair_in.at[i])
            total = keep[i] + pair_in[i].astype(jnp.float32)
            for d in range(chips - 1, 0, -1):
                ret_out[i, d] = total[d].astype(jnp.bfloat16)
            for d in range(chips - 1, 0, -1):
                start("t", i, d)
            own_sum[:, i * width : (i + 1) * width] = total[0]

    for k in range(1, planes):
        diagonal_in("d", k)
    whole(hid_in.at[0], lsem.at[6])
    arrive("h", hid_in.at[pl.ds(1, planes - 1)])
    pieces = [hid_in[k].reshape(local_experts * share, count) for k in range(planes)]
    pieces = jnp.concatenate(pieces, axis=1)
    for k in range(1, planes):
        arrive(("dk", k), every.at[k, pl.ds(0, chips)])
    step = model_width // STEPS
    blocks = step // 128
    for i in range(STEPS):
        result = jnp.dot(
            pieces,
            every[:, :, :, i * step : (i + 1) * step].reshape(planes * count, step),
            preferred_element_type=jnp.float32,
        )
        lines = down_v.at[i].reshape(share * blocks * local_experts, 128)
        for e in range(local_experts):
            for b in range(blocks):
                lines[pl.ds(b * local_experts + e, share, stride=blocks * local_experts), :] = (
                    result[e * share : (e + 1) * share, b * 128 : (b + 1) * 128]
                )
    arrive("t", ret_in)
    sent = sum(
        math.prod(c.src_ref.shape) for key, c in copies.items() if key[0][0] not in ("r", "g")
    )
    whole(wide.at[pl.ds(0, sent // wide.shape[1])], ssem.at[0])
    for i, buf in ((1, rb), (2, gb)):
        whole(buf.at[pl.ds(0, 2 * chips - 1)], ssem.at[i])


def finish_kernel(down_v, own_sum, returned, token_out, down_out, token_v, sems):
    stores = []

    def store(src, dst):
        c = pltpu.make_async_copy(src, dst, sems.at[len(stores)])
        c.start()
        stores.append(c)

    lines = down_v.shape[2]
    for i in range(down_v.shape[0]):
        store(down_v.at[i], down_out.at[:, pl.ds(i * lines, lines)])
    total = own_sum[...]
    for d in range(returned.shape[0]):
        total = total + returned[d].astype(jnp.float32)
    token_v[...] = total.astype(jnp.bfloat16)
    store(token_v, token_out)
    for c in stores:
        c.wait()


def fused_shapes(chips, planes, rows, top, local_experts, model_width, hidden_units):
    bf16, f32 = jnp.bfloat16, jnp.float32
    count, width = 2 * chips * rows, model_width // PARTS
    share = hidden_units // planes
    return [
        ((planes, 2 * chips, rows, model_width), bf16),
        ((planes, local_experts, share, count), bf16),
        ((2 * chips, rows, model_width), bf16),
        ((2 * chips, top, rows), jnp.int32),
        ((2 * chips, top, rows), f32),
        ((model_width, 2 * local_experts * hidden_units), bf16),
        ((local_experts, hidden_units, model_width), bf16),
        ((count, 2 * local_experts * hidden_units), f32),
        ((count, local_experts * hidden_units), f32),
        ((local_experts, hidden_units, count), bf16),
        ((count, 2 * local_experts * hidden_units), bf16),
        ((PARTS, chips, rows, width), f32),
        ((PARTS, chips, rows, width), bf16),
        ((PARTS, chips, rows, width), bf16),
        ((PARTS, chips, rows, width), bf16),
    ]


def buffer_bytes(shapes):
    total = 0
    for dims, kind in shapes:
        size = jnp.dtype(kind).itemsize
        for dim in dims[:-1]:
            size *= dim
        total += size * (-(-dims[-1] // 128) * 128)
    return total


def plan(tokens, routes, w_gate):
    groups, planes = lax.axis_size("expert"), lax.axis_size("dp")
    chips = groups // 2
    rows, model_width = tokens.shape
    local_experts, _, hidden_units = w_gate.shape
    if groups != 8 or planes != 4:
        return None
    if rows % 16 or hidden_units % 128 or (groups * rows) % 128 or model_width % (128 * PARTS):
        return None
    shapes = fused_shapes(
        chips, planes, rows, routes.shape[1], local_experts, model_width, hidden_units
    )
    passed = 4 * hidden_units // planes * local_experts * model_width
    if buffer_bytes(shapes) > VMEM_BUDGET or passed > VMEM_PASSED:
        return None
    return chips, planes, shapes


def shards(tokens, out_grad, routes, route_gates, w_gate, w_up, w_down):
    planned = plan(tokens, routes, w_gate)
    if planned is None:
        return collective_shards(tokens, out_grad, routes, route_gates, w_gate, w_up, w_down)
    chips, planes, shapes = planned
    rows, model_width = tokens.shape
    local_experts, _, hidden_units = w_gate.shape
    share = hidden_units // planes
    amount = len(arrival_groups(planes))
    lines = model_width // STEPS // 128 * local_experts
    outside = pl.BlockSpec(memory_space=pltpu.HBM)
    inside = pl.BlockSpec(memory_space=pltpu.VMEM)
    passed = pl.pallas_call(
        functools.partial(fused_kernel, chips, planes),
        out_shape=(
            pltpu.VMEM((STEPS, share, lines, 128), jnp.float32),
            pltpu.VMEM((rows, model_width), jnp.float32),
            pltpu.VMEM((chips - 1, rows, model_width), jnp.bfloat16),
        ),
        in_specs=[outside] * 7,
        out_specs=(inside,) * 3,
        scratch_shapes=[pltpu.VMEM(dims, kind) for dims, kind in shapes]
        + [
            pltpu.SemaphoreType.DMA((7,)),
            pltpu.SemaphoreType.DMA((3,)),
            pltpu.SemaphoreType.DMA((amount,)),
            pltpu.SemaphoreType.REGULAR,
        ],
        compiler_params=pltpu.CompilerParams(
            collective_id=0, has_side_effects=True, vmem_limit_bytes=VMEM_BUDGET
        ),
        name="expert_backward",
    )(tokens, out_grad, routes.T, route_gates.T, w_gate, w_up, w_down)
    token_grad, down_grad = pl.pallas_call(
        finish_kernel,
        out_shape=(
            jax.ShapeDtypeStruct((rows, model_width), jnp.bfloat16),
            jax.ShapeDtypeStruct((share, model_width // 128 * local_experts, 128), jnp.float32),
        ),
        in_specs=[inside] * 3,
        out_specs=(outside,) * 2,
        scratch_shapes=[
            pltpu.VMEM((rows, model_width), jnp.bfloat16),
            pltpu.SemaphoreType.DMA((1 + STEPS,)),
        ],
        compiler_params=pltpu.CompilerParams(vmem_limit_bytes=32 << 20),
        name="expert_finish",
    )(*passed)
    down_grad = down_grad.reshape(share, model_width // 128, local_experts, 128)
    return (token_grad, down_grad.transpose(0, 2, 1, 3).reshape(share, local_experts, model_width))


def solution(mesh):
    placed = (
        P(("expert", "dp"), None),
        P(("expert", "dp"), None),
        P(("expert", "dp"), None),
        P(("expert", "dp"), None),
        P("expert", None, None),
        P("expert", None, None),
        P("expert", None, None),
    )
    return jax.shard_map(
        shards,
        mesh=mesh,
        in_specs=placed,
        out_specs=(P(("expert", "dp"), None), P("dp", "expert", None)),
        check_vma=False,
    )
```

```python
import functools
import math

import jax
import jax.numpy as jnp
from jax import lax
from jax.experimental import pallas as pl
from jax.experimental.pallas import tpu as pltpu
from jax.sharding import PartitionSpec as P

VMEM_BUDGET = 56 << 20
VMEM_PASSED = 4 << 20
STEPS = 2
PARTS = 4
HALVES = 2
ALONG = ((3, 0), (3, 1))
MESH = pl.DeviceIdType.MESH
NT = (((1,), (1,)), ((), ()))


def gate_up(arrived, w_gate, w_up):
    gate_pre = jnp.einsum("erd,edf->erf", arrived, w_gate, preferred_element_type=jnp.float32)
    up_pre = jnp.einsum("erd,edf->erf", arrived, w_up, preferred_element_type=jnp.float32)
    return (gate_pre, up_pre)


def collective_shards(tokens, out_grad, routes, route_gates, w_gate, w_up, w_down):
    tok_count, model_width = tokens.shape
    top_count = routes.shape[1]
    local_experts = w_gate.shape[0]
    groups = lax.axis_size("expert")
    experts = local_experts * groups
    slot_count = 2 * tok_count * top_count // experts
    flat_routes = routes.reshape(-1)
    onehot = (flat_routes[:, None] == jnp.arange(experts, dtype=jnp.int32)[None, :]).astype(
        jnp.int32
    )
    slot_rank = jnp.sum(onehot * (jnp.cumsum(onehot, axis=0) - onehot), axis=1)
    slot_index = flat_routes * slot_count + slot_rank
    placement = slot_index[None, :] == jnp.arange(experts * slot_count, dtype=jnp.int32)[:, None]
    route_place = placement.astype(jnp.bfloat16)
    token_place = jnp.sum(
        placement.reshape(experts * slot_count, tok_count, top_count).astype(jnp.float32), axis=2
    ).astype(jnp.bfloat16)
    send_inputs = (
        jnp.dot(token_place, tokens, preferred_element_type=jnp.float32)
        .astype(jnp.bfloat16)
        .reshape(experts, slot_count, model_width)
    )
    scaled = (
        (route_gates[:, :, None] * out_grad[:, None, :].astype(jnp.float32))
        .astype(jnp.bfloat16)
        .reshape(tok_count * top_count, model_width)
    )
    send_grads = (
        jnp.dot(route_place, scaled, preferred_element_type=jnp.float32)
        .astype(jnp.bfloat16)
        .reshape(experts, slot_count, model_width)
    )
    arrived, arrived_grad = (
        lax.all_to_all(send_inputs, "expert", split_axis=0, concat_axis=1, tiled=True),
        lax.all_to_all(send_grads, "expert", split_axis=0, concat_axis=1, tiled=True),
    )
    gate_pre, up_pre = gate_up(arrived, w_gate, w_up)
    sigmoid_gate = jax.nn.sigmoid(gate_pre)
    silu_gate = gate_pre * sigmoid_gate
    hidden = (silu_gate * up_pre).astype(jnp.bfloat16)
    hidden_grad = jnp.einsum(
        "erd,efd->erf", arrived_grad, w_down, preferred_element_type=jnp.float32
    )
    gate_grad = (
        hidden_grad * up_pre * (sigmoid_gate + gate_pre * sigmoid_gate * (1.0 - sigmoid_gate))
    ).astype(jnp.bfloat16)
    up_grad = (hidden_grad * silu_gate).astype(jnp.bfloat16)
    row_grads = (
        jnp.einsum("erf,edf->erd", gate_grad, w_gate, preferred_element_type=jnp.float32)
        + jnp.einsum("erf,edf->erd", up_grad, w_up, preferred_element_type=jnp.float32)
    ).astype(jnp.bfloat16)
    returned = lax.all_to_all(row_grads, "expert", split_axis=1, concat_axis=0, tiled=True)
    token_grad = lax.dot_general(
        token_place,
        returned.reshape(experts * slot_count, model_width),
        (((0,), (0,)), ((), ())),
        preferred_element_type=jnp.float32,
    ).astype(jnp.bfloat16)
    hidden_units = hidden.shape[2]
    share_rows = hidden_units // lax.axis_size("dp")
    partial_grad = jnp.einsum(
        "erf,erd->fed", hidden, arrived_grad, preferred_element_type=jnp.float32
    ).astype(jnp.bfloat16)
    total_grad = lax.psum(partial_grad, "dp").astype(jnp.float32)
    first_row = lax.axis_index("dp") * share_rows
    down_grad = lax.dynamic_slice_in_dim(total_grad, first_row, share_rows, 0)
    return (token_grad, down_grad)


def flip(index, bits):
    out, step = index, 1
    while step <= bits:
        if bits & step:
            out = out + step * (1 - 2 * ((index // step) % 2))
        step *= 2
    return out


def arrival_groups(planes):
    names = ["r", "g", "rc", "gc", "h", "t", "first", "xc", "dc"]
    names += [("z", k) for k in range(1, planes)]
    for lead in [("x",)] + [("d", k) for k in range(planes)]:
        names += [lead + (1, 0), lead + (2, 1), lead + ("rest",), lead + (3,)]
    names += [("dk", k) for k in range(1, planes)] + [("p", j) for j in range(PARTS)]
    return {name: i for i, name in enumerate(names)}


def group_of(key):
    name = key[0]
    if name in ("z", "p"):
        return key
    if name in ("r", "g", "rc", "gc", "h", "t"):
        return name
    if name in ("xc", "dc"):
        return "first" if key[:2] == ("xc", 0) else name
    if name == "dk":
        return key[:2]
    d, h = key[-2:]
    lead = key[:-2]
    if d == 3:
        return lead + (3,)
    return lead + ((d, h) if (d, h) in ((1, 0), (2, 1)) else ("rest",))


def fused_kernel(
    chips, planes, tok, dy, rt, gt, wg, wu, wd, down_v, own_sum, ret_in,
    every, hid_in, xb, rb, gb, wide, wdv, pre, grads, hid_out, both,
    keep, pair_out, pair_in, ret_out, lsem, ssem, rsem, known,
):
    local_experts, model_width, hidden_units = wg.shape
    rows = tok.shape[0]
    count = 2 * chips * rows
    share = hidden_units // planes
    width = model_width // PARTS
    half = model_width // HALVES
    me, plane = lax.axis_index("expert"), lax.axis_index("dp")
    chip, core = me // 2, me % 2
    inner = (plane % 2) != (plane // 2)
    partner = {"expert": chip * 2 + 1 - core, "dp": plane}
    across = [{"expert": flip(chip, d) * 2 + core, "dp": plane} for d in range(chips)]
    above = [{"expert": me, "dp": flip(plane, k)} for k in range(planes)]
    groups = arrival_groups(planes)

    def load(src, dst, i):
        c = pltpu.make_async_copy(src, dst, lsem.at[i])
        c.start()
        return c

    own = [
        load(src, dst, i)
        for i, (src, dst) in enumerate(
            ((dy, every.at[0, 0]), (tok, xb.at[0]), (rt, rb.at[0]), (gt, gb.at[0]))
        )
    ]

    def load_weights():
        load(wd, wdv, 4)
        for e in range(local_experts):
            for i, w in enumerate((wg, wu)):
                load(w.at[e], wide.at[:, pl.ds((2 * e + i) * hidden_units, hidden_units)], 5)

    def remote(key, src, dst, target):
        return pltpu.make_async_remote_copy(
            src_ref=src, dst_ref=dst, send_sem=ssem.at[{"r": 1, "g": 2}.get(key[0][0], 0)],
            recv_sem=rsem.at[groups[group_of(key)]], device_id=target, device_id_type=MESH,
        )

    def whole(ref, sem):
        pltpu.make_async_copy(ref, ref, sem).wait()

    def cols(h):
        return pl.ds(h * half, half)

    copies = {}
    for name, src, buf in (("r", rt, rb), ("g", gt, gb)):
        for d in range(chips):
            if d:
                copies[name, d] = remote((name, d), src, buf.at[2 * d], across[d])
            copies[name + "c", d] = remote(
                (name + "c", d), buf.at[2 * d] if d else src, buf.at[2 * d + 1], partner
            )

    def spread(name, first, buf, lead):
        for h in range(HALVES):
            for d in (1, 2):
                copies[(name,) + lead + (d, h)] = remote(
                    (name,) + lead + (d, h), first.at[:, cols(h)], buf.at[2 * d, :, cols(h)], across[d]
                )
            if lead == (1,) and (3, h) in ALONG:
                continue
            via, to = (1, 2) if h == 0 else (2, 1)
            copies[(name,) + lead + (3, h)] = remote(
                (name,) + lead + (3, h), buf.at[2 * via, :, cols(h)], buf.at[6, :, cols(h)], across[to]
            )

    spread("x", tok, xb, ())
    for d in range(chips):
        for h in range(HALVES):
            for key, first, buf in ((("xc",), tok, xb), (("dc",), dy, every.at[0])):
                copies[key + (d, h)] = remote(
                    key + (d, h),
                    buf.at[2 * d, :, cols(h)] if d else first.at[:, cols(h)],
                    buf.at[2 * d + 1, :, cols(h)],
                    partner,
                )
    for k in range(planes):
        spread("d", every.at[k, 0] if k else dy, every.at[k], (k,))
        if k:
            for d in range(chips):
                copies["dk", k, d] = remote(
                    ("dk", k, d), every.at[k, 2 * d], every.at[k, 2 * d + 1], partner
                )
            copies["z", k] = remote(("z", k), dy, every.at[k, 0], above[k])
    for d, h in ALONG:
        copies["d", 1, d, h] = remote(
            ("d", 1, d, h), every.at[0, 2 * d, :, cols(h)], every.at[1, 2 * d, :, cols(h)], above[1]
        )
    for k in range(1, planes):
        first = pl.multiple_of(flip(plane, k) * share, 16)
        for e in range(local_experts):
            copies["h", k, e] = remote(
                ("h", k, e), hid_out.at[e, pl.ds(first, share)], hid_in.at[k, e], above[k]
            )
    for j in range(PARTS):
        copies["p", j] = remote(("p", j), pair_out.at[j], pair_in.at[j], partner)
        for d in range(1, chips):
            copies["t", j, d] = remote(
                ("t", j, d), ret_out.at[j, d], ret_in.at[d - 1, :, pl.ds(j * width, width)], across[d]
            )

    def start(*key):
        copies[key].start()

    def arrive(group, ref):
        whole(ref, rsem.at[groups[group]])

    def place(lead):
        return xb if lead == ("x",) else every.at[lead[1]]

    def relay(*lead):
        for d, h in ((1, 0), (2, 1)):
            arrive(lead + (d, h), place(lead).at[2 * d, :, cols(h)])
            if lead != ("d", 1) or (3, h) not in ALONG:
                start(*lead, 3, h)
            if lead in (("x",), ("d", 0)):
                start(lead[0] + "c", d, h)

    def rest(*lead):
        arrive(lead + ("rest",), place(lead).at[2])
        for d, h in ((1, 1), (2, 0)):
            if lead in (("x",), ("d", 0)):
                start(lead[0] + "c", d, h)
            else:
                start("dk", lead[1], d)

    def diagonal_in(*lead):
        arrive(lead + (3,), place(lead).at[6])
        if lead in (("x",), ("d", 0)):
            for h in range(HALVES):
                start(lead[0] + "c", 3, h)
        else:
            start("dk", lead[1], 3)

    def plane_in(k):
        arrive(("z", k), every.at[k, 0])
        for h in range(HALVES):
            for d in (1, 2):
                start("d", k, d, h if d == 1 else 1 - h)
        start("dk", k, 0)

    barrier = pltpu.get_barrier_semaphore()
    for target in [partner] + across[1:3] + [above[1]]:
        pl.semaphore_signal(barrier, inc=1, device_id=target, device_id_type=MESH)

    @pl.when(inner)
    def _():
        pl.semaphore_signal(barrier, inc=1, device_id=above[3], device_id_type=MESH)

    pl.semaphore_wait(barrier, 4 + inner.astype(jnp.int32))

    @pl.when(inner)
    def _():
        pl.semaphore_signal(known, inc=1, device_id=above[3], device_id_type=MESH)
        copies["z", 3].start()

    def send_own(*lead):
        for h in range(HALVES):
            for d in (1, 2):
                start(*lead, d, h if d == 1 else 1 - h)
        for h in range(HALVES):
            start(lead[0] + "c", 0, h)

    send_own("x")
    start("z", 1)
    for name in ("r", "g"):
        for d in (1, 2):
            start(name, d)
        start(name + "c", 0)
    load_weights()
    arrive("first", xb.at[1])
    send_own("d", 0)

    @pl.when(inner)
    def _():
        pl.semaphore_wait(known, 1)
        pl.semaphore_signal(known, inc=1, device_id=above[1], device_id_type=MESH)
        copies["z", 2].start()

    relay("x")
    for name in ("r", "g"):
        start(name, 3)

    @pl.when(jnp.logical_not(inner))
    def _():
        pl.semaphore_wait(known, 1)
        copies["z", 3].start()
        copies["z", 2].start()

    rest("x")
    relay("d", 0)
    rest("d", 0)
    for c in own:
        c.wait()
    diagonal_in("x")
    for name, buf in (("r", rb), ("g", gb)):
        arrive(name, buf.at[pl.ds(0, chips - 1)])
        for d in range(1, chips):
            start(name + "c", d)
    diagonal_in("d", 0)
    for d, h in ALONG:
        start("d", 1, d, h)
    plane_in(1)

    whole(wide, lsem.at[5])
    arrive("xc", xb.at[pl.ds(0, chips - 1)])
    pre[...] = jnp.dot(
        xb[...].reshape(count, model_width), wide[...], preferred_element_type=jnp.float32
    )
    plane_in(2)
    arrive("rc", rb.at[pl.ds(0, chips)])
    arrive("gc", gb.at[pl.ds(0, chips)])

    named, given = rb[...], gb[...]
    diagonal = lax.broadcasted_iota(jnp.int32, (1, rows, rows), 1) == lax.broadcasted_iota(
        jnp.int32, (1, rows, rows), 2
    )
    for e in range(local_experts):
        gain = jnp.sum(
            jnp.where(named == me * local_experts + e, given, 0.0), axis=1, keepdims=True
        )
        gain = jnp.sum(jnp.where(diagonal, gain, 0.0), axis=2, keepdims=True).reshape(count, 1)
        a, b, c = ((2 * e + i) * hidden_units for i in range(3))
        gate_pre, up_pre = pre[:, a:b], pre[:, b:c]
        s = jax.nn.sigmoid(gate_pre)
        silu = gate_pre * s * gain
        hid_out[e] = (silu * up_pre).T.astype(jnp.bfloat16)
        pre[:, a:b] = up_pre * (s + gate_pre * s * (1.0 - s)) * gain
        pre[:, b:c] = silu
    for k in range(planes - 1, 0, -1):
        for e in range(local_experts):
            start("h", k, e)
    first = pl.multiple_of(plane * share, 16)
    for e in range(local_experts):
        load(hid_out.at[e, pl.ds(first, share)], hid_in.at[0, e], 6)

    whole(wdv, lsem.at[4])
    arrive("dc", every.at[0, pl.ds(0, chips)])
    grads[...] = lax.dot_general(
        every[0].reshape(count, model_width),
        wdv[...].reshape(local_experts * hidden_units, model_width),
        NT,
        preferred_element_type=jnp.float32,
    )
    plane_in(3)
    relay("d", 1)
    rest("d", 1)
    for e in range(local_experts):
        hidden_grad = grads[:, e * hidden_units : (e + 1) * hidden_units]
        for i in (2 * e, 2 * e + 1):
            part = slice(i * hidden_units, (i + 1) * hidden_units)
            both[:, part] = (hidden_grad * pre[:, part]).astype(jnp.bfloat16)

    for j in range(PARTS + 1):
        if j < PARTS:
            total = lax.dot_general(
                both[...], wide[j * width : (j + 1) * width, :], NT, preferred_element_type=jnp.float32
            ).reshape(chips, 2, rows, width)
            pair_out[j] = total[:, 1].astype(jnp.bfloat16)
            start("p", j)
            keep[j] = total[:, 0]
        if j == 0:
            relay("d", 2)
        if j == 2:
            relay("d", 3)
            rest("d", 2)
        if j == 3:
            rest("d", 3)
        if j:
            i = j - 1
            arrive(("p", i), pair_in.at[i])
            total = keep[i] + pair_in[i].astype(jnp.float32)
            for d in range(chips - 1, 0, -1):
                ret_out[i, d] = total[d].astype(jnp.bfloat16)
            for d in range(chips - 1, 0, -1):
                start("t", i, d)
            own_sum[:, i * width : (i + 1) * width] = total[0]

    for k in range(1, planes):
        diagonal_in("d", k)
    whole(hid_in.at[0], lsem.at[6])
    arrive("h", hid_in.at[pl.ds(1, planes - 1)])
    pieces = [hid_in[k].reshape(local_experts * share, count) for k in range(planes)]
    pieces = jnp.concatenate(pieces, axis=1)
    for k in range(1, planes):
        arrive(("dk", k), every.at[k, pl.ds(0, chips)])
    step = model_width // STEPS
    blocks = step // 128
    for i in range(STEPS):
        result = jnp.dot(
            pieces,
            every[:, :, :, i * step : (i + 1) * step].reshape(planes * count, step),
            preferred_element_type=jnp.float32,
        )
        lines = down_v.at[i].reshape(share * blocks * local_experts, 128)
        for e in range(local_experts):
            for b in range(blocks):
                lines[pl.ds(b * local_experts + e, share, stride=blocks * local_experts), :] = (
                    result[e * share : (e + 1) * share, b * 128 : (b + 1) * 128]
                )
    arrive("t", ret_in)
    sent = sum(
        math.prod(c.src_ref.shape) for key, c in copies.items() if key[0][0] not in ("r", "g")
    )
    whole(wide.at[pl.ds(0, sent // wide.shape[1])], ssem.at[0])
    for i, buf in ((1, rb), (2, gb)):
        whole(buf.at[pl.ds(0, 2 * chips - 1)], ssem.at[i])


def finish_kernel(down_v, own_sum, returned, token_out, down_out, token_v, sems):
    stores = []

    def store(src, dst):
        c = pltpu.make_async_copy(src, dst, sems.at[len(stores)])
        c.start()
        stores.append(c)

    lines = down_v.shape[2]
    for i in range(down_v.shape[0]):
        store(down_v.at[i], down_out.at[:, pl.ds(i * lines, lines)])
    total = own_sum[...]
    for d in range(returned.shape[0]):
        total = total + returned[d].astype(jnp.float32)
    token_v[...] = total.astype(jnp.bfloat16)
    store(token_v, token_out)
    for c in stores:
        c.wait()


def fused_shapes(chips, planes, rows, top, local_experts, model_width, hidden_units):
    bf16, f32 = jnp.bfloat16, jnp.float32
    count, width = 2 * chips * rows, model_width // PARTS
    share = hidden_units // planes
    return [
        ((planes, 2 * chips, rows, model_width), bf16),
        ((planes, local_experts, share, count), bf16),
        ((2 * chips, rows, model_width), bf16),
        ((2 * chips, top, rows), jnp.int32),
        ((2 * chips, top, rows), f32),
        ((model_width, 2 * local_experts * hidden_units), bf16),
        ((local_experts, hidden_units, model_width), bf16),
        ((count, 2 * local_experts * hidden_units), f32),
        ((count, local_experts * hidden_units), f32),
        ((local_experts, hidden_units, count), bf16),
        ((count, 2 * local_experts * hidden_units), bf16),
        ((PARTS, chips, rows, width), f32),
        ((PARTS, chips, rows, width), bf16),
        ((PARTS, chips, rows, width), bf16),
        ((PARTS, chips, rows, width), bf16),
    ]


def buffer_bytes(shapes):
    total = 0
    for dims, kind in shapes:
        size = jnp.dtype(kind).itemsize
        for dim in dims[:-1]:
            size *= dim
        total += size * (-(-dims[-1] // 128) * 128)
    return total


def plan(tokens, routes, w_gate):
    groups, planes = lax.axis_size("expert"), lax.axis_size("dp")
    chips = groups // 2
    rows, model_width = tokens.shape
    local_experts, _, hidden_units = w_gate.shape
    if groups != 8 or planes != 4:
        return None
    if rows % 16 or hidden_units % 128 or (groups * rows) % 128 or model_width % (128 * PARTS):
        return None
    shapes = fused_shapes(
        chips, planes, rows, routes.shape[1], local_experts, model_width, hidden_units
    )
    passed = 4 * hidden_units // planes * local_experts * model_width
    if buffer_bytes(shapes) > VMEM_BUDGET or passed > VMEM_PASSED:
        return None
    return chips, planes, shapes


def shards(tokens, out_grad, routes, route_gates, w_gate, w_up, w_down):
    planned = plan(tokens, routes, w_gate)
    if planned is None:
        return collective_shards(tokens, out_grad, routes, route_gates, w_gate, w_up, w_down)
    chips, planes, shapes = planned
    rows, model_width = tokens.shape
    local_experts, _, hidden_units = w_gate.shape
    share = hidden_units // planes
    amount = len(arrival_groups(planes))
    lines = model_width // STEPS // 128 * local_experts
    outside = pl.BlockSpec(memory_space=pltpu.HBM)
    inside = pl.BlockSpec(memory_space=pltpu.VMEM)
    passed = pl.pallas_call(
        functools.partial(fused_kernel, chips, planes),
        out_shape=(
            pltpu.VMEM((STEPS, share, lines, 128), jnp.float32),
            pltpu.VMEM((rows, model_width), jnp.float32),
            pltpu.VMEM((chips - 1, rows, model_width), jnp.bfloat16),
        ),
        in_specs=[outside] * 7,
        out_specs=(inside,) * 3,
        scratch_shapes=[pltpu.VMEM(dims, kind) for dims, kind in shapes]
        + [
            pltpu.SemaphoreType.DMA((7,)),
            pltpu.SemaphoreType.DMA((3,)),
            pltpu.SemaphoreType.DMA((amount,)),
            pltpu.SemaphoreType.REGULAR,
        ],
        compiler_params=pltpu.CompilerParams(
            collective_id=0, has_side_effects=True, vmem_limit_bytes=VMEM_BUDGET
        ),
        name="expert_backward",
    )(tokens, out_grad, routes.T, route_gates.T, w_gate, w_up, w_down)
    token_grad, down_grad = pl.pallas_call(
        finish_kernel,
        out_shape=(
            jax.ShapeDtypeStruct((rows, model_width), jnp.bfloat16),
            jax.ShapeDtypeStruct((share, model_width // 128 * local_experts, 128), jnp.float32),
        ),
        in_specs=[inside] * 3,
        out_specs=(outside,) * 2,
        scratch_shapes=[
            pltpu.VMEM((rows, model_width), jnp.bfloat16),
            pltpu.SemaphoreType.DMA((1 + STEPS,)),
        ],
        compiler_params=pltpu.CompilerParams(vmem_limit_bytes=32 << 20),
        name="expert_finish",
    )(*passed)
    down_grad = down_grad.reshape(share, model_width // 128, local_experts, 128)
    return (token_grad, down_grad.transpose(0, 2, 1, 3).reshape(share, local_experts, model_width))


def solution(mesh):
    placed = (
        P(("expert", "dp"), None),
        P(("expert", "dp"), None),
        P(("expert", "dp"), None),
        P(("expert", "dp"), None),
        P("expert", None, None),
        P("expert", None, None),
        P("expert", None, None),
    )
    return jax.shard_map(
        shards,
        mesh=mesh,
        in_specs=placed,
        out_specs=(P(("expert", "dp"), None), P("dp", "expert", None)),
        check_vma=False,
    )
```
